32 devices in a mesh: groups: 2 (over y), gx: 4 (over z), samples: 2 (over x), gy: 2 (over core).
Axes of the slice: x: 2, y: 2, z: 4, core: 2. Of those that a mesh axis runs over, the one named last changes fastest.
Arguments:
- seeds: int32 [16], P(('groups', 'samples')), parts along dimension 0, may hold values from 0 to 63
- wind_profiles: float32 [64, 3, 128], replicated, may hold values from 0.04 to 0.16
- gust: float32 [32, 128, 128], P('gx', 'gy'), may hold values from 0.5 to 1.5
- reaction: float32 [32, 128, 128], P('gx', 'gy'), may hold values from 0.05 to 0.25
- flags: int32 [16, 32, 128, 128], P(('groups', 'samples'), 'gx', 'gy'), parts along dimension 0, may hold values from 0 to 7
- mask: int32 [32, 128], P('gx', 'gy'), may hold values 0 or 1
- kernel: float32 [128], replicated, may hold values from -0.5 to 0.5
- states: bfloat16 [5, 16, 32, 128, 128], P(None, ('groups', 'samples'), 'gx', 'gy'), parts along dimension 1, may hold values from -4 to 4
Outputs:
- risk_map: float32 [64, 128], P(('groups', 'gx'), 'gy'), parts along dimension 0
- source_gradient: float32 [64, 128, 128], P(('groups', 'gx', 'samples'), 'gy'), parts along dimension 0
- initial_adjoint: float32 [16, 32, 128, 128], P(('groups', 'samples'), 'gx', 'gy'), parts along dimension 0
The draws below stay inside these ranges and needn't reach their ends.
There are 2 independent parts, one for each index of `groups`. The reference program is written for one: setup_inputs(seed, part) draws one part's arguments, and reference() takes and returns one part's arrays. A program takes and returns all parts, laid end to end along the dimension named above; an argument that names none is the same for every part. Nothing has to cross between parts.
Inputs may be any that keep to these rules, and one draw needn't show every extreme that they name: `seeds`: each seed names a row of wind_profiles. `flags`: bit d of a flag is 1 where the cell's outflow along dimension d goes toward higher indices.
All inputs are finite; a program needn't handle non-finite values. No bound on the sum of `mask` on one device may be relied on, other than what follows from the above.
Results may differ from the reference program's by a relative error of at most 0.0003.
Values may be sent and summed in bfloat16 or wider, within the bound.
No kernel may reach another device: no remote copies, remote signals or barrier semaphores. Data moves between devices by JAX's collectives and lax.ppermute only.
A program may use at most 64 MiB of HBM per device.

```python
import math
import jax
import jax.numpy as jnp
from jax import lax

NZ = 128
STEPS = 4
NPROF = 64
S = 8
NX = 32
NY = 128


def place_ends(array, stream_key, low, top_value):
    longest = array.shape.index(max(array.shape))
    spots = []
    for shift in (0, 1):
        where = [jax.random.randint(jax.random.fold_in(stream_key, axis), (), 0, length) for axis, length in enumerate(array.shape)]
        where[longest] = (where[longest] + shift) % array.shape[longest]
        spots.append(tuple(where))
    return array.at[spots[0]].set(low).at[spots[1]].set(top_value)


def steps_of(rng, dims, split, smallest, largest):
    factor_of, own = 1.0, jax.random.fold_in(rng, 6)
    for position, shards_of in split:
        heights = jnp.exp(jax.random.uniform(jax.random.fold_in(own, position), (shards_of,), jnp.float32, smallest / len(split), largest / len(split)))
        factor_of = factor_of * jnp.repeat(heights, dims[position] // shards_of).reshape([-1 if axis == position else 1 for axis in range(len(dims))])
    return factor_of


def centred(stream_key, extent, deviation, reach, split=(), held_as=jnp.bfloat16):
    gain = steps_of(stream_key, extent, split, -0.22, 0.18) if split else 1.0
    array = jax.random.normal(stream_key, extent, jnp.float32) * deviation * gain
    return jnp.minimum(jnp.maximum(array, -reach), reach).astype(held_as)


def setup_inputs(seed: int = 0, part: int = 0) -> dict:
    key_of = jax.random.split(jax.random.key(seed), 9)
    own_keys = jax.random.split(jax.random.fold_in(key_of[8], part), 9)
    return {
        "seeds": place_ends(jax.random.randint(own_keys[0], (S,), 0, NPROF), jax.random.fold_in(own_keys[0], 1), 0, NPROF - 1).astype(jnp.int32),
        "wind_profiles": jnp.clip(jax.random.uniform(key_of[1], (NPROF, 3, NZ), jnp.float32, 0.04, 0.16), 0.04, 0.16),
        "gust": jnp.clip(jnp.exp(math.log(1.5) - 1.0986123 * jax.random.uniform(key_of[2], (NX, NY, NZ), jnp.float32) ** steps_of(key_of[2], (NX, NY, NZ), ((0, 4), (1, 2)), -0.2, 0.2)), 0.5, 1.5),
        "reaction": jnp.clip(jnp.exp(math.log(0.25) - 1.609438 * jax.random.uniform(key_of[3], (NX, NY, NZ), jnp.float32) ** steps_of(key_of[3], (NX, NY, NZ), ((0, 4), (1, 2)), -0.2, 0.2)), 0.05, 0.25),
        "flags": place_ends(jax.random.randint(own_keys[4], (S, NX, NY, NZ), 0, 8), jax.random.fold_in(own_keys[4], 1), 0, 7).astype(jnp.int32),
        "mask": place_ends((jax.random.randint(key_of[5], (NX, NY), 0, 2) < 1).astype(jnp.int32), jax.random.fold_in(key_of[5], 1), 0, 1),
        "kernel": centred(key_of[6], (NZ,), NZ ** -0.5, 0.5, (), jnp.float32),
        "states": centred(own_keys[7], (STEPS + 1, S, NX, NY, NZ), 1.0, 4.0, ((1, 2), (2, 4), (3, 2))),
    }


DIFFUSION = 0.05
KURTOSIS_WEIGHT = 1.0


def bit_value(outflow_bits, component):
    return ((outflow_bits // (2 ** component)) % 2).astype(jnp.float32)


def outflow_rates(profile, outflow_bits, gust):
    rates = []
    for component in range(3):
        speeds = profile[component] * gust
        toward = bit_value(outflow_bits, component)
        rates.append(speeds * toward)
        rates.append(speeds * (1.0 - toward))
    return rates


def vertical(adjoint, upward, downward):
    zero_rim = jnp.zeros(adjoint.shape[:-1] + (1,), jnp.float32)
    above = jnp.concatenate([adjoint[..., 1:], zero_rim], -1)
    below = jnp.concatenate([zero_rim, adjoint[..., :-1]], -1)
    rising = jnp.concatenate([adjoint[..., 1:] - adjoint[..., :-1], zero_rim], -1)
    falling = jnp.concatenate([zero_rim, adjoint[..., :-1] - adjoint[..., 1:]], -1)
    return upward * above + downward * below + DIFFUSION * (rising + falling)


def adjoint_step(adjoint, stored, rates, leaving, reaction):
    east_out, west_out, north_out, south_out, upward, downward = rates
    east_side = jnp.roll(adjoint, -1, axis=0)
    west_side = jnp.roll(adjoint, 1, axis=0)
    padded_second = jnp.pad(adjoint, ((0, 0), (1, 1), (0, 0)))
    mixed = (1.0 - leaving) * adjoint + east_out * east_side + west_out * west_side
    mixed = mixed + north_out * padded_second[:, 2:] + south_out * padded_second[:, :-2]
    return mixed + vertical(adjoint, upward, downward) - 2.0 * reaction * stored * adjoint


def reference(seeds, wind_profiles, gust, reaction, flags, mask, kernel, states):
    sample_count = seeds.shape[0]
    receptor = mask.astype(jnp.float32)
    surface = jnp.sum(states[STEPS].astype(jnp.float32) * kernel, axis=-1)
    average = jnp.sum(surface, axis=0) / sample_count
    spread = surface - average
    third_moment = jnp.sum(spread ** 3, axis=0) / sample_count
    fourth_moment = jnp.sum(spread ** 4, axis=0) / sample_count
    risk_map = receptor * (average + KURTOSIS_WEIGHT * fourth_moment)
    sensitivity = receptor * (1.0 / sample_count + (4.0 * KURTOSIS_WEIGHT / sample_count) * (spread ** 3 - third_moment))
    profiles = wind_profiles[seeds]
    history = jnp.moveaxis(states[:STEPS], 1, 0)

    def one_sample(sample_items):
        profile, outflow_bits, final_sense, stored_run = sample_items
        rates = outflow_rates(profile, outflow_bits, gust)
        leaving = rates[0] + rates[1] + rates[2] + rates[3] + rates[4] + rates[5]
        adjoint = final_sense[:, :, None] * kernel
        running = adjoint
        for back_step in range(STEPS - 1, -1, -1):
            adjoint = adjoint_step(adjoint, stored_run[back_step].astype(jnp.float32), rates, leaving, reaction)
            if back_step > 0:
                running = running + adjoint
        return adjoint, running

    initial_adjoint, totals = lax.map(one_sample, (profiles, flags, sensitivity, history))
    return risk_map, jnp.sum(totals, axis=0), initial_adjoint
```

```python
import functools

import jax
import jax.numpy as jnp
from jax import lax
from jax.experimental import pallas as pl
from jax.experimental.pallas import tpu as pltpu
from jax.sharding import PartitionSpec as P

STEPS = 4
DIFFUSION = 0.05
KURTOSIS_WEIGHT = 1.0

F32 = jnp.float32
BF16 = jnp.bfloat16
VMEM = pl.BlockSpec(memory_space=pltpu.VMEM)
ANY = pl.BlockSpec(memory_space=pl.ANY)


def call(body, outs, args, name, out_specs=None, in_specs=None, scratch=(), aliases=None, micros=1.0):
    return pl.pallas_call(
        body,
        name=name,
        out_shape=outs,
        in_specs=in_specs or [VMEM] * len(args),
        out_specs=out_specs or jax.tree.map(lambda _: VMEM, outs),
        scratch_shapes=scratch,
        input_output_aliases=aliases or {},
        compiler_params=pltpu.CompilerParams(vmem_limit_bytes=4 << 20),
        cost_estimate=pl.CostEstimate(
            flops=int(1e6 * micros), bytes_accessed=int(3e6 * micros), transcendentals=0
        ),
    )(*args)


def shape(*dims, dtype=F32):
    return jax.ShapeDtypeStruct(dims, dtype)


def three_parts(value):
    first = value.astype(BF16).astype(F32)
    second = (value - first).astype(BF16).astype(F32)
    third = value - first - second
    return first, second, third


def stack_rows(rows, width):
    index = lax.broadcasted_iota(jnp.int32, (16, width), 0)
    block = jnp.zeros((16, width), F32)
    for position, row in enumerate(rows):
        block = jnp.where(index == position, row, block)
    return block.astype(BF16)


def surface_body(states_ref, kernel_ref, out_ref):
    samples, rows, width, levels = states_ref.shape
    parts = stack_rows(three_parts(kernel_ref[...]), levels)
    for k in range(samples):
        flat = states_ref[k].reshape(rows * width, levels)
        product = lax.dot_general(
            parts, flat, (((1,), (1,)), ((), ())), preferred_element_type=F32
        )
        out_ref[k : k + 1] = product[0:1] + product[1:2] + product[2:3]


def outer_rows(row, kernel_rows):
    first, second, third = three_parts(row)
    left = stack_rows((first, first, first, second, second, third), row.shape[1])
    return lax.dot_general(
        left, kernel_rows, (((0,), (0,)), ((), ())), preferred_element_type=F32
    )


def kernel_rows_of(kernel_ref):
    first, second, third = three_parts(kernel_ref[...])
    return stack_rows((first, second, third, first, second, first), kernel_ref.shape[1])


def final_body(sens_ref, beside_ref, kernel_ref, side_ref, edge_ref, inner_ref, beside_out, run_edge_ref, run_inner_ref):
    samples, _, width, levels = edge_ref.shape
    rows = inner_ref.shape[1] + 2
    right = kernel_rows_of(kernel_ref)
    total = [jnp.zeros((width, levels), F32)] * rows
    lanes = lax.broadcasted_iota(jnp.int32, (rows, rows * width), 1)
    starts = lax.broadcasted_iota(jnp.int32, (rows, rows * width), 0) * width
    wanted = lanes == starts + jnp.where(side_ref[0, 0] > 0.5, width - 1, 0)
    for k in range(samples):
        block = outer_rows(sens_ref[k : k + 1], right)
        for x in range(rows):
            piece = block[x * width : (x + 1) * width]
            if x == 0:
                edge_ref[k, 0] = piece
            elif x == rows - 1:
                edge_ref[k, 1] = piece
            else:
                inner_ref[k, x - 1] = piece
            total[x] = total[x] + piece
        column = jnp.sum(jnp.where(wanted, beside_ref[k : k + 1], 0.0), axis=1, keepdims=True)
        beside_out[k] = column * kernel_ref[...]
    run_edge_ref[0] = total[0]
    run_edge_ref[1] = total[rows - 1]
    for x in range(1, rows - 1):
        run_inner_ref[x - 1] = total[x]


def halo_body(low_ref, high_ref, kernel_ref, low_out, high_out):
    right = kernel_rows_of(kernel_ref)
    for source, target in ((low_ref, low_out), (high_ref, high_out)):
        for k in range(target.shape[0]):
            target[k] = outer_rows(source[k : k + 1], right)


class Plan:
    def __init__(self, levels):
        lane = lax.broadcasted_iota(jnp.int32, (8, levels), 1)
        row = lax.broadcasted_iota(jnp.int32, (8, levels), 0)
        self.below_top = lane < levels - 1
        self.above_base = lane > 0
        self.top_row = row == 7
        self.base_row = row == 0
        self.loss = 1.0 - (
            jnp.where(self.below_top, DIFFUSION, 0.0) + jnp.where(self.above_base, DIFFUSION, 0.0)
        )


def step_row(plan, centre, west, east, low_row, high_row, bits, gust, twice, stored, speeds):
    width, levels = centre.shape
    tiles = width // 8
    first, second, third, whole = speeds
    piece = lambda value, t: value[8 * t : 8 * t + 8]
    parts = [piece(centre, t) for t in range(tiles)]
    up = [pltpu.roll(part, 7, 0) for part in parts] + [jnp.broadcast_to(high_row, (8, levels))]
    down = [jnp.broadcast_to(low_row, (8, levels))] + [pltpu.roll(part, 1, 0) for part in parts]
    result = []
    for t in range(tiles):
        here = parts[t]
        north = jnp.where(plan.top_row, up[t + 1], up[t])
        south = jnp.where(plan.base_row, down[t], down[t + 1])
        above = jnp.where(plan.below_top, pltpu.roll(here, levels - 1, 1), 0.0)
        below = jnp.where(plan.above_base, pltpu.roll(here, 1, 1), 0.0)
        flag = piece(bits, t)
        moved = (
            first * jnp.where((flag & 1) != 0, piece(east, t), piece(west, t))
            + second * jnp.where((flag & 2) != 0, north, south)
            + third * jnp.where((flag & 4) != 0, above, below)
            - whole * here
        )
        result.append(
            here * (plan.loss - piece(twice, t) * piece(stored, t))
            + piece(gust, t) * moved
            + DIFFUSION * (above + below)
        )
    return result


def speeds_of(profile_ref, k, levels):
    rows = [profile_ref[k, d : d + 1] for d in range(3)]
    rows.append(rows[0] + rows[1] + rows[2])
    return [jnp.broadcast_to(row, (8, levels)) for row in rows]


def inner_body(
    step, last, edge_ref, inner_ref, beside_ref, side_ref, run_ref, flags_ref, gust_ref, reaction_ref,
    states_ref, profile_ref, *outs
):
    samples, inside, width, levels = inner_ref.shape
    plan = Plan(levels)
    if last:
        target, buffer, semaphore = outs
    else:
        buffer, run_out = outs

    def at(k, x):
        return edge_ref[k, x // (inside + 1)] if x in (0, inside + 1) else inner_ref[k, x - 1]

    for x in range(1, inside + 1):
        gust = gust_ref[x]
        twice = 2.0 * reaction_ref[x]
        total = None if last else [run_ref[x - 1, 8 * t : 8 * t + 8] for t in range(width // 8)]
        for k in range(samples):
            halo = beside_ref[k, x : x + 1]
            tiles = step_row(
                plan, at(k, x), at(k, x - 1), at(k, x + 1), halo * side_ref[0:1], halo * side_ref[1:2],
                flags_ref[k, x], gust, twice, states_ref[step, k, x].astype(F32),
                speeds_of(profile_ref, k, levels),
            )
            for t, tile in enumerate(tiles):
                buffer[k, x - 1, 8 * t : 8 * t + 8] = tile
                if not last:
                    total[t] = total[t] + tile
        if not last:
            for t, tile in enumerate(total):
                run_out[x - 1, 8 * t : 8 * t + 8] = tile
    if last:
        copy = pltpu.make_async_copy(buffer, target.at[:, 1 : inside + 1], semaphore)
        copy.start()
        copy.wait()


def edge_body(
    step, last, edge_ref, inner_ref, low_ref, high_ref, beside_ref, side_ref, run_ref, flags_ref, gust_ref,
    reaction_ref, states_ref, profile_ref, now_ref, *outs
):
    samples, inside, width, levels = inner_ref.shape
    plan = Plan(levels)
    if last:
        target, buffer, semaphore = outs
    else:
        buffer, low_out, high_out, beside_out, run_out = outs
    for side, x in enumerate((0, inside + 1)):
        gust = gust_ref[x]
        twice = 2.0 * reaction_ref[x]
        total = None if last else [run_ref[side, 8 * t : 8 * t + 8] for t in range(width // 8)]
        for k in range(samples):
            halo = beside_ref[k, x : x + 1]
            if side == 0:
                west, east = low_ref[k].astype(F32), inner_ref[k, 0]
            else:
                west, east = inner_ref[k, inside - 1], high_ref[k].astype(F32)
            tiles = step_row(
                plan, edge_ref[k, side], west, east, halo * side_ref[0:1], halo * side_ref[1:2],
                flags_ref[k, x], gust, twice, states_ref[step, k, x].astype(F32),
                speeds_of(profile_ref, k, levels),
            )
            for t, tile in enumerate(tiles):
                buffer[k, side, 8 * t : 8 * t + 8] = tile
                if not last:
                    total[t] = total[t] + tile
            if not last:
                whole = jnp.concatenate(tiles, axis=0).astype(BF16)
                (low_out if side == 0 else high_out)[k] = whole
                rim = jnp.where(side_ref[0:1] > 0.5, tiles[0][0:1], tiles[-1][7:8])
                beside_out[k, x : x + 1] = rim
        if not last:
            for t, tile in enumerate(total):
                run_out[side, 8 * t : 8 * t + 8] = tile
    if last:
        copies = [
            pltpu.make_async_copy(buffer.at[:, 0], target.at[:, 0], semaphore.at[0]),
            pltpu.make_async_copy(buffer.at[:, 1], target.at[:, inside + 1], semaphore.at[1]),
        ]
        for copy in copies:
            copy.start()
        for copy in copies:
            copy.wait()
    else:
        for k in range(samples):
            for x in range(1, inside + 1):
                rim = jnp.where(side_ref[0:1] > 0.5, now_ref[k, x - 1, 0:1], now_ref[k, x - 1, width - 1 : width])
                beside_out[k, x : x + 1] = rim


def exchange_x(to_low, to_high):
    count = lax.axis_size("gx")
    forward = [(i, (i + 1) % count) for i in range(count)]
    backward = [(target, source) for source, target in forward]
    return lax.ppermute(to_high, "gx", forward), lax.ppermute(to_low, "gx", backward)


def swap_y(block):
    return lax.ppermute(block, "gy", [(0, 1), (1, 0)])


def on_device(seeds, wind_profiles, gust, reaction, flags, mask, kernel, states):
    local_count, rows, width, levels = flags.shape
    shards = lax.axis_size("samples")
    sample_count = local_count * shards
    inside = rows - 2
    kernel_row = kernel[None, :]
    side = jnp.broadcast_to(
        jnp.stack([lax.axis_index("gy") == 1, lax.axis_index("gy") == 0]).astype(F32)[:, None], (2, levels)
    )

    surface = call(
        surface_body, shape(local_count, rows * width), (states[STEPS], kernel_row), "surface"
    )
    others = [
        lax.ppermute(surface, "samples", [(i, (i + hop) % shards) for i in range(shards)])
        for hop in range(1, shards)
    ]
    every = jnp.concatenate([surface] + others, axis=0)
    receptor = mask.reshape(1, rows * width).astype(F32)
    average = jnp.sum(every, axis=0, keepdims=True) / sample_count
    spread = every - average
    cubed = spread * spread * spread
    third_moment = jnp.sum(cubed, axis=0, keepdims=True) / sample_count
    fourth_moment = jnp.sum(cubed * spread, axis=0, keepdims=True) / sample_count
    risk_map = (receptor * (average + KURTOSIS_WEIGHT * fourth_moment)).reshape(rows, width)
    sensitivity = receptor * (
        1.0 / sample_count
        + 4.0 * KURTOSIS_WEIGHT / sample_count * (cubed[:local_count] - third_moment)
    )

    profile_table = wind_profiles.reshape(wind_profiles.shape[0], -1)
    selector = (seeds[:, None] == jnp.arange(profile_table.shape[0], dtype=jnp.int32)[None, :]).astype(F32)
    profile = jnp.dot(
        selector, profile_table, precision=lax.Precision.HIGHEST, preferred_element_type=F32
    ).reshape(local_count, 3, levels)

    low_sens, high_sens = exchange_x(sensitivity[:, :width], sensitivity[:, (rows - 1) * width :])
    beside_sens = swap_y(sensitivity)
    edge, inner, beside, run_edge, run_inner = call(
        final_body,
        (
            shape(local_count, 2, width, levels),
            shape(local_count, inside, width, levels),
            shape(local_count, rows, levels),
            shape(2, width, levels),
            shape(inside, width, levels),
        ),
        (sensitivity, beside_sens, kernel_row, side),
        "final",
    )
    low, high = call(
        halo_body, (shape(local_count, width, levels),) * 2, (low_sens, high_sens, kernel_row), "halo"
    )
    fixed = (flags, gust, reaction, states, profile)
    for step in range(STEPS - 1, 0, -1):
        inner_now, run_inner = call(
            functools.partial(inner_body, step, False),
            (shape(local_count, inside, width, levels), shape(inside, width, levels)),
            (edge, inner, beside, side, run_inner) + fixed,
            f"inner{step}",
        )
        edge_now, to_low, to_high, to_beside, run_edge = call(
            functools.partial(edge_body, step, False),
            (
                shape(local_count, 2, width, levels),
                shape(local_count, width, levels, dtype=BF16),
                shape(local_count, width, levels, dtype=BF16),
                shape(local_count, rows, levels),
                shape(2, width, levels),
            ),
            (edge, inner, low, high, beside, side, run_edge) + fixed + (inner_now,),
            f"edge{step}",
            micros=0.4,
        )
        edge, inner = edge_now, inner_now
        low, high = exchange_x(to_low, to_high)
        beside = swap_y(to_beside)

    target = call(
        functools.partial(inner_body, 0, True),
        shape(*flags.shape),
        (edge, inner, beside, side, run_inner) + fixed,
        "inner0",
        out_specs=ANY,
        scratch=[pltpu.VMEM((local_count, inside, width, levels), F32), pltpu.SemaphoreType.DMA],
    )
    running = jnp.concatenate([run_edge[:1], run_inner, run_edge[1:]], axis=0)
    share_rows = rows // shards
    me = lax.axis_index("samples")
    source_gradient = lax.dynamic_slice_in_dim(running, me * share_rows, share_rows, 0)
    for hop in range(1, shards):
        to = (me + hop) % shards
        piece = lax.dynamic_slice_in_dim(running, to * share_rows, share_rows, 0)
        source_gradient = source_gradient + lax.ppermute(
            piece, "samples", [(i, (i + hop) % shards) for i in range(shards)]
        )
    args = (edge, inner, low, high, beside, side, run_edge) + fixed + (target,)
    initial_adjoint = call(
        functools.partial(edge_body, 0, True),
        shape(*flags.shape),
        args,
        "edge0",
        out_specs=ANY,
        in_specs=[VMEM] * (len(args) - 1) + [ANY],
        scratch=[pltpu.VMEM((local_count, 2, width, levels), F32), pltpu.SemaphoreType.DMA((2,))],
        aliases={len(args) - 1: 0},
        micros=0.4,
    )
    return risk_map, source_gradient, initial_adjoint


def solution(mesh):
    return jax.shard_map(
        on_device,
        mesh=mesh,
        in_specs=(
            P(("groups", "samples")),
            P(),
            P("gx", "gy", None),
            P("gx", "gy", None),
            P(("groups", "samples"), "gx", "gy", None),
            P("gx", "gy"),
            P(),
            P(None, ("groups", "samples"), "gx", "gy", None),
        ),
        out_specs=(
            P(("groups", "gx"), "gy"),
            P(("groups", "gx", "samples"), "gy", None),
            P(("groups", "samples"), "gx", "gy", None),
        ),
        check_vma=False,
    )
```

```python
import functools

import jax
import jax.numpy as jnp
from jax import lax
from jax.experimental import pallas as pl
from jax.experimental.pallas import tpu as pltpu
from jax.sharding import PartitionSpec as P

STEPS = 4
DIFFUSION = 0.05
KURTOSIS_WEIGHT = 1.0

F32 = jnp.float32
BF16 = jnp.bfloat16
VMEM = pl.BlockSpec(memory_space=pltpu.VMEM)
ANY = pl.BlockSpec(memory_space=pl.ANY)
HBM = pl.BlockSpec(memory_space=pltpu.HBM)


def call(body, outs, args, name, out_specs=None, in_specs=None, scratch=(), aliases=None, micros=1.0):
    return pl.pallas_call(
        body,
        name=name,
        out_shape=outs,
        in_specs=in_specs or [VMEM] * len(args),
        out_specs=out_specs or jax.tree.map(lambda _: VMEM, outs),
        scratch_shapes=scratch,
        input_output_aliases=aliases or {},
        compiler_params=pltpu.CompilerParams(vmem_limit_bytes=4 << 20),
        cost_estimate=pl.CostEstimate(
            flops=int(1e6 * micros), bytes_accessed=int(3e6 * micros), transcendentals=0
        ),
    )(*args)


def shape(*dims, dtype=F32):
    return jax.ShapeDtypeStruct(dims, dtype)


def three_parts(value):
    first = value.astype(BF16).astype(F32)
    second = (value - first).astype(BF16).astype(F32)
    third = value - first - second
    return first, second, third


def stack_rows(rows, width):
    index = lax.broadcasted_iota(jnp.int32, (16, width), 0)
    block = jnp.zeros((16, width), F32)
    for position, row in enumerate(rows):
        block = jnp.where(index == position, row, block)
    return block.astype(BF16)


def surface_body(states_ref, kernel_ref, mask_ref, surface_ref, kernel_out, mask_out, buffer, semaphores):
    samples, rows, width, levels = buffer.shape
    head = [
        pltpu.make_async_copy(kernel_ref, kernel_out, semaphores.at[samples]),
        pltpu.make_async_copy(mask_ref, mask_out, semaphores.at[samples + 1]),
    ]
    copies = [
        pltpu.make_async_copy(states_ref.at[STEPS, k], buffer.at[k], semaphores.at[k])
        for k in range(samples)
    ]
    for copy in head + copies:
        copy.start()
    head[0].wait()
    parts = stack_rows(three_parts(kernel_out[...]), levels)
    for k in range(samples):
        copies[k].wait()
        for x in range(rows):
            product = lax.dot_general(
                parts, buffer[k, x], (((1,), (1,)), ((), ())), preferred_element_type=F32
            )
            surface_ref[k, x : x + 1] = product[0:1] + product[1:2] + product[2:3]
    head[1].wait()


def moments_body(count, *refs):
    parts, mask_ref = refs[:count], refs[count]
    risk_ref, sens_ref, low_ref, high_ref = refs[count + 1 :]
    samples, rows, _ = sens_ref.shape
    total = samples * count
    every = [part[k] for part in parts for k in range(samples)]
    average = sum(every) / total
    spread = [value - average for value in every]
    cubed = [value * value * value for value in spread]
    third_moment = sum(cubed) / total
    fourth_moment = sum(cube * value for cube, value in zip(cubed, spread)) / total
    receptor = mask_ref[...].astype(F32)
    risk_ref[...] = receptor * (average + KURTOSIS_WEIGHT * fourth_moment)
    for k in range(samples):
        sens = receptor * (
            1.0 / total + 4.0 * KURTOSIS_WEIGHT / total * (cubed[k] - third_moment)
        )
        sens_ref[k] = sens
        low_ref[k : k + 1] = sens[0:1]
        high_ref[k : k + 1] = sens[rows - 1 : rows]


def outer_rows(row, kernel_rows):
    first, second, third = three_parts(row)
    left = stack_rows((first, first, first, second, second, third), row.shape[1])
    return lax.dot_general(
        left, kernel_rows, (((0,), (0,)), ((), ())), preferred_element_type=F32
    )


def kernel_rows_of(kernel_ref):
    first, second, third = three_parts(kernel_ref[...])
    return stack_rows((first, second, third, first, second, first), kernel_ref.shape[1])


def final_body(sens_ref, beside_ref, kernel_ref, edge_ref, inner_ref, beside_out, run_edge_ref, run_inner_ref):
    samples, rows, width = sens_ref.shape
    levels = kernel_ref.shape[1]
    right = kernel_rows_of(kernel_ref)
    lanes = lax.broadcasted_iota(jnp.int32, (rows, width), 1)
    wanted = lanes == jnp.where(lax.axis_index("gy") == 1, width - 1, 0)
    for k in range(samples):
        column = jnp.sum(jnp.where(wanted, beside_ref[k], 0.0), axis=1, keepdims=True)
        beside_out[k] = column * kernel_ref[...]
    for x in range(rows):
        total = jnp.zeros((width, levels), F32)
        for k in range(samples):
            piece = outer_rows(sens_ref[k, x : x + 1], right)
            if x in (0, rows - 1):
                edge_ref[k, x // (rows - 1)] = piece
            else:
                inner_ref[k, x - 1] = piece
            total = total + piece
        if x in (0, rows - 1):
            run_edge_ref[x // (rows - 1)] = total
        else:
            run_inner_ref[x - 1] = total


def halo_body(low_ref, high_ref, kernel_ref, low_out, high_out):
    right = kernel_rows_of(kernel_ref)
    for source, target in ((low_ref, low_out), (high_ref, high_out)):
        for k in range(target.shape[0]):
            target[k] = outer_rows(source[k : k + 1], right)


def load_body(
    seeds_ref, table_ref, flags_ref, gust_ref, reaction_ref, states_ref,
    profile_out, flags_out, gust_out, reaction_out, states_out, table, semaphores
):
    samples = flags_out.shape[0]
    copies = [(table_ref, table), (gust_ref, gust_out), (reaction_ref, reaction_out)]
    for k in range(samples):
        copies.append((flags_ref.at[k], flags_out.at[k]))
    for step in reversed(range(STEPS)):
        copies.append((states_ref.at[step], states_out.at[step]))
    copies = [
        pltpu.make_async_copy(source, target, semaphores.at[i])
        for i, (source, target) in enumerate(copies)
    ]
    for copy in copies:
        copy.start()
    copies[0].wait()
    for k in range(samples):
        for d in range(3):
            profile_out[k, d : d + 1] = table[d, pl.ds(seeds_ref[k], 1)]
    for copy in copies[1:]:
        copy.wait()


class Plan:
    def __init__(self, levels):
        lane = lax.broadcasted_iota(jnp.int32, (8, levels), 1)
        row = lax.broadcasted_iota(jnp.int32, (8, levels), 0)
        self.below_top = lane < levels - 1
        self.above_base = lane > 0
        self.top_row = row == 7
        self.base_row = row == 0
        self.loss = 1.0 - (
            jnp.where(self.below_top, DIFFUSION, 0.0) + jnp.where(self.above_base, DIFFUSION, 0.0)
        )


def step_row(plan, centre, west, east, low_row, high_row, bits, gust, twice, stored, speeds):
    width, levels = centre.shape
    tiles = width // 8
    first, second, third, whole = speeds
    piece = lambda value, t: value[8 * t : 8 * t + 8]
    parts = [piece(centre, t) for t in range(tiles)]
    up = [pltpu.roll(part, 7, 0) for part in parts] + [jnp.broadcast_to(high_row, (8, levels))]
    down = [jnp.broadcast_to(low_row, (8, levels))] + [pltpu.roll(part, 1, 0) for part in parts]
    result = []
    for t in range(tiles):
        here = parts[t]
        north = jnp.where(plan.top_row, up[t + 1], up[t])
        south = jnp.where(plan.base_row, down[t], down[t + 1])
        above = jnp.where(plan.below_top, pltpu.roll(here, levels - 1, 1), 0.0)
        below = jnp.where(plan.above_base, pltpu.roll(here, 1, 1), 0.0)
        flag = piece(bits, t)
        moved = (
            first * jnp.where((flag & 1) != 0, piece(east, t), piece(west, t))
            + second * jnp.where((flag & 2) != 0, north, south)
            + third * jnp.where((flag & 4) != 0, above, below)
            - whole * here
        )
        result.append(
            here * (plan.loss - piece(twice, t) * piece(stored, t))
            + piece(gust, t) * moved
            + DIFFUSION * (above + below)
        )
    return result


def speeds_of(profile_ref, k, levels):
    rows = [profile_ref[k, d : d + 1] for d in range(3)]
    rows.append(rows[0] + rows[1] + rows[2])
    return [jnp.broadcast_to(row, (8, levels)) for row in rows]


def side_flags(levels):
    side = lax.axis_index("gy")
    ones = jnp.full((1, levels), 1.0, F32)
    return jnp.where(side == 1, ones, 0.0), jnp.where(side == 0, ones, 0.0), side == 1


def inner_body(
    step, last, edge_ref, inner_ref, beside_ref, run_ref, profile_ref, flags_ref, gust_ref, reaction_ref,
    states_ref, *outs
):
    samples, inside, width, levels = inner_ref.shape
    plan = Plan(levels)
    if last:
        target, buffer, semaphores = outs
    else:
        buffer, rim_out, run_out = outs
    low_side, high_side, upper = side_flags(levels)
    copies = []

    def at(k, x):
        return edge_ref[k, x // (inside + 1)] if x in (0, inside + 1) else inner_ref[k, x - 1]

    for x in range(1, inside + 1):
        gust = gust_ref[x]
        twice = 2.0 * reaction_ref[x]
        total = None if last else [run_ref[x - 1, 8 * t : 8 * t + 8] for t in range(width // 8)]
        for k in range(samples):
            halo = beside_ref[k, x : x + 1]
            tiles = step_row(
                plan, at(k, x), at(k, x - 1), at(k, x + 1), halo * low_side, halo * high_side,
                flags_ref[k, x], gust, twice, states_ref[step, k, x].astype(F32),
                speeds_of(profile_ref, k, levels),
            )
            for t, tile in enumerate(tiles):
                buffer[k, x - 1, 8 * t : 8 * t + 8] = tile
                if not last:
                    total[t] = total[t] + tile
            if not last:
                rim_out[k, x : x + 1] = jnp.where(upper, tiles[0][0:1], tiles[-1][7:8])
        if last:
            copies.append(
                pltpu.make_async_copy(buffer.at[:, x - 1], target.at[:, x], semaphores.at[x - 1])
            )
            copies[-1].start()
        else:
            for t, tile in enumerate(total):
                run_out[x - 1, 8 * t : 8 * t + 8] = tile
    for copy in copies:
        copy.wait()


def edge_body(
    step, last, rims, edge_ref, inner_ref, low_ref, high_ref, beside_ref, run_ref, profile_ref, flags_ref,
    gust_ref, reaction_ref, states_ref, *outs
):
    samples, inside, width, levels = inner_ref.shape
    plan = Plan(levels)
    copies = []
    if last:
        pieces, (_, target, source_out, buffer, source, semaphores) = outs[:rims], outs[rims:]
        source[...] = sum(piece[...] for piece in pieces)
        copies.append(pltpu.make_async_copy(source, source_out, semaphores.at[2]))
        copies[-1].start()
    else:
        buffer, low_out, high_out, rim_out, run_out = outs
    low_side, high_side, upper = side_flags(levels)
    for side, x in enumerate((0, inside + 1)):
        gust = gust_ref[x]
        twice = 2.0 * reaction_ref[x]
        total = None if last else [run_ref[side, 8 * t : 8 * t + 8] for t in range(width // 8)]
        for k in range(samples):
            row = side if beside_ref.shape[1] == 2 else x
            halo = beside_ref[k, row : row + 1]
            if side == 0:
                west, east = low_ref[k].astype(F32), inner_ref[k, 0]
            else:
                west, east = inner_ref[k, inside - 1], high_ref[k].astype(F32)
            tiles = step_row(
                plan, edge_ref[k, side], west, east, halo * low_side, halo * high_side,
                flags_ref[k, x], gust, twice, states_ref[step, k, x].astype(F32),
                speeds_of(profile_ref, k, levels),
            )
            for t, tile in enumerate(tiles):
                buffer[k, side, 8 * t : 8 * t + 8] = tile
                if not last:
                    total[t] = total[t] + tile
            if not last:
                whole = jnp.concatenate(tiles, axis=0).astype(BF16)
                (low_out if side == 0 else high_out)[k] = whole
                rim_out[k, side : side + 1] = jnp.where(upper, tiles[0][0:1], tiles[-1][7:8])
        if last:
            copies.append(
                pltpu.make_async_copy(buffer.at[:, side], target.at[:, x], semaphores.at[side])
            )
            copies[-1].start()
        else:
            for t, tile in enumerate(total):
                run_out[side, 8 * t : 8 * t + 8] = tile
    for copy in copies:
        copy.wait()


def share_body(shards, edge_ref, inner_ref, *outs):
    pieces, full = outs[:shards], outs[shards]
    rows = full.shape[0]
    full[0] = edge_ref[0]
    full[1 : rows - 1] = inner_ref[...]
    full[rows - 1] = edge_ref[1]
    me = lax.axis_index("samples")
    share = rows // shards
    for hop in range(shards):
        owner = lax.rem(me + hop, shards)
        pieces[hop][...] = full[pl.ds(owner * share, share)]


def exchange_x(to_low, to_high):
    count = lax.axis_size("gx")
    forward = [(i, (i + 1) % count) for i in range(count)]
    backward = [(target, source) for source, target in forward]
    return lax.ppermute(to_high, "gx", forward), lax.ppermute(to_low, "gx", backward)


def swap_y(block):
    return lax.ppermute(block, "gy", [(0, 1), (1, 0)])


def rotate(block, axis, hop):
    count = lax.axis_size(axis)
    return lax.ppermute(block, axis, [(i, (i + hop) % count) for i in range(count)])


def on_device(seeds, wind_profiles, gust, reaction, flags, mask, kernel, states):
    local_count, rows, width, levels = flags.shape
    shards = lax.axis_size("samples")
    inside = rows - 2
    slab = shape(local_count, width, levels)
    hold = lambda value: pltpu.with_memory_space_constraint(value, pltpu.HBM)
    flags, gust, reaction, states, mask = map(hold, (flags, gust, reaction, states, mask))
    kernel = hold(kernel[None, :])
    table = hold(jnp.swapaxes(wind_profiles, 0, 1))

    surface, kernel_row, mask_here = call(
        surface_body,
        (shape(local_count, rows, width), shape(1, levels), shape(rows, width, dtype=jnp.int32)),
        (states, kernel, mask),
        "surface",
        in_specs=[HBM] * 3,
        scratch=[
            pltpu.VMEM((local_count, rows, width, levels), BF16),
            pltpu.SemaphoreType.DMA((local_count + 2,)),
        ],
    )
    others = [rotate(surface, "samples", hop) for hop in range(1, shards)]
    risk_map, sensitivity, low_sens, high_sens = call(
        functools.partial(moments_body, shards),
        (shape(rows, width), shape(local_count, rows, width)) + (shape(local_count, width),) * 2,
        (surface, *others, mask_here),
        "moments",
        micros=0.1,
    )
    low, high = exchange_x(low_sens, high_sens)
    beside_sens = swap_y(sensitivity)
    fixed = call(
        load_body,
        (
            shape(local_count, 3, levels),
            shape(*flags.shape, dtype=flags.dtype),
            shape(*gust.shape),
            shape(*reaction.shape),
            shape(STEPS, *flags.shape, dtype=states.dtype),
        ),
        (seeds, table, flags, gust, reaction, states),
        "load",
        in_specs=[pl.BlockSpec(memory_space=pltpu.SMEM)] + [HBM] * 5,
        scratch=[
            pltpu.VMEM((3, wind_profiles.shape[0], levels), F32),
            pltpu.SemaphoreType.DMA((local_count + 3 + STEPS,)),
        ],
    )
    edge, inner, beside, run_edge, run_inner = call(
        final_body,
        (
            shape(local_count, 2, width, levels),
            shape(local_count, inside, width, levels),
            shape(local_count, rows, levels),
            shape(2, width, levels),
            shape(inside, width, levels),
        ),
        (sensitivity, beside_sens, kernel_row),
        "final",
        micros=0.3,
    )
    beside_edge = beside
    low, high = call(halo_body, (slab,) * 2, (low, high, kernel_row), "halo", micros=0.1)
    for step in range(STEPS - 1, 0, -1):
        inner_now, rim_inner, run_inner = call(
            functools.partial(inner_body, step, False),
            (
                shape(local_count, inside, width, levels),
                shape(local_count, rows, levels),
                shape(inside, width, levels),
            ),
            (edge, inner, beside, run_inner) + fixed,
            f"inner{step}",
        )
        edge, to_low, to_high, rim_edge, run_edge = call(
            functools.partial(edge_body, step, False, 0),
            (
                shape(local_count, 2, width, levels),
                shape(local_count, width, levels, dtype=BF16),
                shape(local_count, width, levels, dtype=BF16),
                shape(local_count, 2, levels),
                shape(2, width, levels),
            ),
            (edge, inner, low, high, beside_edge, run_edge) + fixed,
            f"edge{step}",
            micros=0.4,
        )
        inner = inner_now
        low, high = exchange_x(to_low, to_high)
        beside, beside_edge = swap_y(rim_inner), swap_y(rim_edge)

    target = call(
        functools.partial(inner_body, 0, True),
        shape(*flags.shape),
        (edge, inner, beside, run_inner) + fixed,
        "inner0",
        out_specs=ANY,
        scratch=[pltpu.VMEM((local_count, inside, width, levels), F32), pltpu.SemaphoreType.DMA((inside,))],
    )
    share = shape(rows // shards, width, levels)
    pieces = call(
        functools.partial(share_body, shards),
        (share,) * shards,
        (run_edge, run_inner),
        "share",
        scratch=[pltpu.VMEM((rows, width, levels), F32)],
        micros=0.1,
    )
    pieces = [pieces[0]] + [rotate(pieces[hop], "samples", hop) for hop in range(1, shards)]
    args = (edge, inner, low, high, beside_edge, run_edge) + fixed + (*pieces, target)
    initial_adjoint, source_gradient = call(
        functools.partial(edge_body, 0, True, shards),
        (shape(*flags.shape), share),
        args,
        "edge0",
        out_specs=(ANY, ANY),
        in_specs=[VMEM] * (len(args) - 1) + [ANY],
        scratch=[
            pltpu.VMEM((local_count, 2, width, levels), F32),
            pltpu.VMEM(share.shape, F32),
            pltpu.SemaphoreType.DMA((3,)),
        ],
        aliases={len(args) - 1: 0},
        micros=0.4,
    )
    return risk_map, source_gradient, initial_adjoint


def solution(mesh):
    return jax.shard_map(
        on_device,
        mesh=mesh,
        in_specs=(
            P(("groups", "samples")),
            P(),
            P("gx", "gy", None),
            P("gx", "gy", None),
            P(("groups", "samples"), "gx", "gy", None),
            P("gx", "gy"),
            P(),
            P(None, ("groups", "samples"), "gx", "gy", None),
        ),
        out_specs=(
            P(("groups", "gx"), "gy"),
            P(("groups", "gx", "samples"), "gy", None),
            P(("groups", "samples"), "gx", "gy", None),
        ),
        check_vma=False,
    )
```

```python
import functools

import jax
import jax.numpy as jnp
from jax import lax
from jax.experimental import pallas as pl
from jax.experimental.pallas import tpu as pltpu
from jax.sharding import PartitionSpec as P

STEPS = 4
DIFFUSION = 0.05
KURTOSIS_WEIGHT = 1.0
INNER_COST = 1.0

F32 = jnp.float32
BF16 = jnp.bfloat16
VMEM = pl.BlockSpec(memory_space=pltpu.VMEM)
ANY = pl.BlockSpec(memory_space=pl.ANY)
HBM = pl.BlockSpec(memory_space=pltpu.HBM)


def call(body, outs, args, name, out_specs=None, in_specs=None, scratch=(), aliases=None, micros=1.0):
    return pl.pallas_call(
        body,
        name=name,
        out_shape=outs,
        in_specs=in_specs or [VMEM] * len(args),
        out_specs=out_specs or jax.tree.map(lambda _: VMEM, outs),
        scratch_shapes=scratch,
        input_output_aliases=aliases or {},
        compiler_params=pltpu.CompilerParams(vmem_limit_bytes=4 << 20),
        cost_estimate=pl.CostEstimate(
            flops=int(1e6 * micros), bytes_accessed=int(3e6 * micros), transcendentals=0
        ),
    )(*args)


def shape(*dims, dtype=F32):
    return jax.ShapeDtypeStruct(dims, dtype)


def three_parts(value):
    first = value.astype(BF16).astype(F32)
    second = (value - first).astype(BF16).astype(F32)
    third = value - first - second
    return first, second, third


def stack_rows(rows, width):
    index = lax.broadcasted_iota(jnp.int32, (16, width), 0)
    block = jnp.zeros((16, width), F32)
    for position, row in enumerate(rows):
        block = jnp.where(index == position, row, block)
    return block.astype(BF16)


def surface_body(states_ref, kernel_ref, surface_ref, kernel_out, buffer, semaphores):
    samples, rows, width, levels = buffer.shape
    copies = [
        pltpu.make_async_copy(states_ref.at[STEPS, k], buffer.at[k], semaphores.at[k])
        for k in range(samples)
    ]
    copies.append(pltpu.make_async_copy(kernel_ref, kernel_out, semaphores.at[samples]))
    for copy in copies:
        copy.start()
    copies[-1].wait()
    parts = stack_rows(three_parts(kernel_out[...]), levels)
    for k in range(samples):
        copies[k].wait()
        flat = buffer[k].reshape(rows * width, levels)
        product = lax.dot_general(
            parts, flat, (((1,), (1,)), ((), ())), preferred_element_type=F32
        )
        surface_ref[k : k + 1] = product[0:1] + product[1:2] + product[2:3]


def load_body(
    seeds_ref, flags_ref, gust_ref, reaction_ref, states_ref, mask_ref, table_ref, _,
    profile_out, flags_out, gust_out, reaction_out, stored_out, receptor_out, mask, table, padded, semaphores
):
    samples, rows, width, levels = flags_out.shape
    pairs = [(table_ref, table), (mask_ref, mask), (gust_ref, gust_out), (reaction_ref, reaction_out)]
    pairs += [(flags_ref.at[k], flags_out.at[k]) for k in range(samples)]
    pairs += [(states_ref.at[step], stored_out.at[step]) for step in range(STEPS)]
    copies = [
        pltpu.make_async_copy(source, target, semaphores.at[i]) for i, (source, target) in enumerate(pairs)
    ]
    for copy in copies:
        copy.start()
    copies[0].wait()
    for k in range(samples):
        for d in range(3):
            profile_out[k, d : d + 1] = table[d, pl.ds(seeds_ref[k], 1)]
    copies[1].wait()
    padded[...] = jnp.zeros_like(padded)
    padded[:, :width] = mask[...].astype(F32)
    for pair in range(rows // 2):
        receptor_out[:, 2 * width * pair : 2 * width * (pair + 1)] = (
            padded[2 * pair : 2 * pair + 1] + pltpu.roll(padded[2 * pair + 1 : 2 * pair + 2], width, 1)
        )
    for copy in copies[2:]:
        copy.wait()


def moments_body(count, *refs):
    parts, receptor_ref = refs[:count], refs[count]
    risk_ref, sens_ref, low_ref, high_ref = refs[count + 2 :]
    samples, cells = sens_ref.shape
    width = low_ref.shape[1]
    total = samples * count
    fold = lambda values: sum(jnp.sum(value, axis=0, keepdims=True) for value in values) / total
    every = [part[...] for part in parts]
    average = fold(every)
    spread = [value - average for value in every]
    cubed = [value * value * value for value in spread]
    third_moment = fold(cubed)
    fourth_moment = fold([cube * value for cube, value in zip(cubed, spread)])
    receptor = receptor_ref[...]
    risk_ref[...] = receptor * (average + KURTOSIS_WEIGHT * fourth_moment)
    sens = receptor * (1.0 / total + 4.0 * KURTOSIS_WEIGHT / total * (cubed[0] - third_moment))
    sens_ref[...] = sens
    low_ref[...] = sens[:, :width]
    high_ref[...] = pltpu.roll(sens[:, cells - 2 * width :], width, 1)[:, :width]


def outer_rows(row, kernel_rows):
    first, second, third = three_parts(row)
    left = stack_rows((first, first, first, second, second, third), row.shape[1])
    return lax.dot_general(
        left, kernel_rows, (((0,), (0,)), ((), ())), preferred_element_type=F32
    )


def kernel_rows_of(kernel_ref):
    first, second, third = three_parts(kernel_ref[...])
    return stack_rows((first, second, third, first, second, first), kernel_ref.shape[1])


def final_body(sens_ref, beside_ref, kernel_ref, edge_ref, inner_ref, beside_out, run_edge_ref, run_inner_ref):
    samples, inside, width, levels = inner_ref.shape
    rows = inside + 2
    right = kernel_rows_of(kernel_ref)
    total = [jnp.zeros((width, levels), F32)] * rows
    lanes = lax.broadcasted_iota(jnp.int32, (rows, rows * width), 1)
    starts = lax.broadcasted_iota(jnp.int32, (rows, rows * width), 0) * width
    wanted = lanes == starts + jnp.where(lax.axis_index("gy") == 1, width - 1, 0)
    for k in range(samples):
        block = outer_rows(sens_ref[k : k + 1], right)
        for x in range(rows):
            piece = block[x * width : (x + 1) * width]
            if x in (0, rows - 1):
                edge_ref[k, x // (rows - 1)] = piece
            else:
                inner_ref[k, x - 1] = piece
            total[x] = total[x] + piece
        column = jnp.sum(jnp.where(wanted, beside_ref[k : k + 1], 0.0), axis=1, keepdims=True)
        beside_out[k] = column * kernel_ref[...]
    run_edge_ref[0] = total[0]
    run_edge_ref[1] = total[rows - 1]
    for x in range(1, rows - 1):
        run_inner_ref[x - 1] = total[x]


def halo_body(low_ref, high_ref, kernel_ref, _, low_out, high_out):
    right = kernel_rows_of(kernel_ref)
    for source, target in ((low_ref, low_out), (high_ref, high_out)):
        for k in range(target.shape[0]):
            target[k] = outer_rows(source[k : k + 1], right)


class Plan:
    def __init__(self, levels):
        lane = lax.broadcasted_iota(jnp.int32, (8, levels), 1)
        row = lax.broadcasted_iota(jnp.int32, (8, levels), 0)
        self.below_top = lane < levels - 1
        self.above_base = lane > 0
        self.top_row = row == 7
        self.base_row = row == 0
        self.loss = 1.0 - (
            jnp.where(self.below_top, DIFFUSION, 0.0) + jnp.where(self.above_base, DIFFUSION, 0.0)
        )


def step_row(plan, centre, west, east, low_row, high_row, bits, gust, twice, stored, speeds):
    width, levels = centre.shape
    tiles = width // 8
    first, second, third, whole = speeds
    piece = lambda value, t: value[8 * t : 8 * t + 8]
    parts = [piece(centre, t) for t in range(tiles)]
    up = [pltpu.roll(part, 7, 0) for part in parts] + [jnp.broadcast_to(high_row, (8, levels))]
    down = [jnp.broadcast_to(low_row, (8, levels))] + [pltpu.roll(part, 1, 0) for part in parts]
    result = []
    for t in range(tiles):
        here = parts[t]
        north = jnp.where(plan.top_row, up[t + 1], up[t])
        south = jnp.where(plan.base_row, down[t], down[t + 1])
        above = jnp.where(plan.below_top, pltpu.roll(here, levels - 1, 1), 0.0)
        below = jnp.where(plan.above_base, pltpu.roll(here, 1, 1), 0.0)
        flag = piece(bits, t)
        moved = (
            first * jnp.where((flag & 1) != 0, piece(east, t), piece(west, t))
            + second * jnp.where((flag & 2) != 0, north, south)
            + third * jnp.where((flag & 4) != 0, above, below)
            - whole * here
        )
        result.append(
            here * (plan.loss - piece(twice, t) * piece(stored, t))
            + piece(gust, t) * moved
            + DIFFUSION * (above + below)
        )
    return result


def speeds_of(profile_ref, k, levels):
    rows = [profile_ref[k, d : d + 1] for d in range(3)]
    rows.append(rows[0] + rows[1] + rows[2])
    return [jnp.broadcast_to(row, (8, levels)) for row in rows]


def side_flags(levels):
    side = lax.axis_index("gy")
    ones = jnp.full((1, levels), 1.0, F32)
    return jnp.where(side == 1, ones, 0.0), jnp.where(side == 0, ones, 0.0), side == 1


def inner_body(
    step, last, edge_ref, inner_ref, beside_ref, run_ref, profile_ref, flags_ref, gust_ref, reaction_ref,
    stored_ref, *outs
):
    samples, inside, width, levels = inner_ref.shape
    plan = Plan(levels)
    if last:
        risk_ref, buffer, risk_out = outs
        for x in range(inside + 2):
            pair = risk_ref[:, 2 * width * (x // 2) : 2 * width * (x // 2 + 1)]
            pair = pair if x % 2 == 0 else pltpu.roll(pair, width, 1)
            risk_out[x : x + 1] = pair[:, :width]
    else:
        buffer, rim_out, run_out = outs
    low_side, high_side, upper = side_flags(levels)

    def at(k, x):
        return edge_ref[k, x // (inside + 1)] if x in (0, inside + 1) else inner_ref[k, x - 1]

    for x in range(1, inside + 1):
        gust = gust_ref[x]
        twice = 2.0 * reaction_ref[x]
        total = None if last else [run_ref[x - 1, 8 * t : 8 * t + 8] for t in range(width // 8)]
        for k in range(samples):
            halo = beside_ref[k, x : x + 1]
            tiles = step_row(
                plan, at(k, x), at(k, x - 1), at(k, x + 1), halo * low_side, halo * high_side,
                flags_ref[k, x], gust, twice, stored_ref[step, k, x].astype(F32),
                speeds_of(profile_ref, k, levels),
            )
            for t, tile in enumerate(tiles):
                buffer[k, x - 1, 8 * t : 8 * t + 8] = tile
                if not last:
                    total[t] = total[t] + tile
            if not last:
                rim_out[k, x : x + 1] = jnp.where(upper, tiles[0][0:1], tiles[-1][7:8])
        if not last:
            for t, tile in enumerate(total):
                run_out[x - 1, 8 * t : 8 * t + 8] = tile


def edge_body(
    step, last, shards, edge_ref, inner_ref, low_ref, high_ref, beside_ref, run_ref, profile_ref, flags_ref,
    gust_ref, reaction_ref, stored_ref, *outs
):
    samples, inside, width, levels = inner_ref.shape
    plan = Plan(levels)
    copies = []
    if last:
        pieces, (now_ref, target, source_out, buffer, source, semaphores) = outs[:shards], outs[shards:]
        for k in range(samples):
            copies.append(
                pltpu.make_async_copy(
                    now_ref.at[k], target.at[k, 1 : inside + 1], semaphores.at[2 * samples + 1 + k]
                )
            )
            copies[-1].start()
        source[...] = sum(piece[...] for piece in pieces)
        copies.append(pltpu.make_async_copy(source, source_out, semaphores.at[2 * samples]))
        copies[-1].start()
    else:
        rim_ref, buffer, low_out, high_out, rim_out, run_out = outs
        rim_out[...] = rim_ref[...]
    low_side, high_side, upper = side_flags(levels)
    for side, x in enumerate((0, inside + 1)):
        gust = gust_ref[x]
        twice = 2.0 * reaction_ref[x]
        total = None if last else [run_ref[side, 8 * t : 8 * t + 8] for t in range(width // 8)]
        for k in range(samples):
            halo = beside_ref[k, x : x + 1]
            if side == 0:
                west, east = low_ref[k].astype(F32), inner_ref[k, 0]
            else:
                west, east = inner_ref[k, inside - 1], high_ref[k].astype(F32)
            tiles = step_row(
                plan, edge_ref[k, side], west, east, halo * low_side, halo * high_side,
                flags_ref[k, x], gust, twice, stored_ref[step, k, x].astype(F32),
                speeds_of(profile_ref, k, levels),
            )
            for t, tile in enumerate(tiles):
                buffer[k, side, 8 * t : 8 * t + 8] = tile
                if not last:
                    total[t] = total[t] + tile
            if not last:
                whole = jnp.concatenate(tiles, axis=0).astype(BF16)
                (low_out if side == 0 else high_out)[k] = whole
                rim_out[k, x : x + 1] = jnp.where(upper, tiles[0][0:1], tiles[-1][7:8])
            if last:
                copies.append(
                    pltpu.make_async_copy(
                        buffer.at[k, side], target.at[k, x], semaphores.at[side * samples + k]
                    )
                )
                copies[-1].start()
        if not last:
            for t, tile in enumerate(total):
                run_out[side, 8 * t : 8 * t + 8] = tile
    for copy in copies:
        copy.wait()


def share_body(shards, edge_ref, inner_ref, _, *outs):
    pieces, full = outs[:shards], outs[shards]
    rows = full.shape[0]
    full[0] = edge_ref[0]
    full[1 : rows - 1] = inner_ref[...]
    full[rows - 1] = edge_ref[1]
    me = lax.axis_index("samples")
    share = rows // shards
    for hop in range(shards):
        owner = lax.rem(me + hop, shards)
        pieces[hop][...] = full[pl.ds(owner * share, share)]


def exchange_x(to_low, to_high):
    count = lax.axis_size("gx")
    forward = [(i, (i + 1) % count) for i in range(count)]
    backward = [(target, source) for source, target in forward]
    return lax.ppermute(to_high, "gx", forward), lax.ppermute(to_low, "gx", backward)


def swap_y(block):
    return lax.ppermute(block, "gy", [(0, 1), (1, 0)])


def rotate(block, axis, hop):
    count = lax.axis_size(axis)
    return lax.ppermute(block, axis, [(i, (i + hop) % count) for i in range(count)])


def on_device(seeds, wind_profiles, gust, reaction, flags, mask, kernel, states):
    local_count, rows, width, levels = flags.shape
    shards = lax.axis_size("samples")
    inside = rows - 2
    slab = shape(local_count, width, levels)
    rim = shape(local_count, rows, levels)
    flat = shape(local_count, rows * width)
    hold = lambda value: pltpu.with_memory_space_constraint(value, pltpu.HBM)
    states = hold(states)

    surface, kernel_row = call(
        surface_body,
        (flat, shape(1, levels)),
        (states, hold(kernel[None, :])),
        "surface",
        in_specs=[HBM] * 2,
        scratch=[
            pltpu.VMEM((local_count, rows, width, levels), BF16),
            pltpu.SemaphoreType.DMA((local_count + 1,)),
        ],
    )
    table = jnp.swapaxes(wind_profiles, 0, 1)
    *fixed, receptor = call(
        load_body,
        (
            shape(local_count, 3, levels),
            shape(*flags.shape, dtype=flags.dtype),
            shape(*gust.shape),
            shape(*reaction.shape),
            shape(STEPS, *flags.shape, dtype=states.dtype),
            shape(1, rows * width),
        ),
        (seeds, hold(flags), hold(gust), hold(reaction), states, hold(mask), hold(table), kernel_row),
        "load",
        in_specs=[pl.BlockSpec(memory_space=pltpu.SMEM)] + [HBM] * 6 + [VMEM],
        scratch=[
            pltpu.VMEM(mask.shape, mask.dtype),
            pltpu.VMEM(table.shape, F32),
            pltpu.VMEM((rows, 2 * width), F32),
            pltpu.SemaphoreType.DMA((local_count + STEPS + 4,)),
        ],
    )
    others = [rotate(surface, "samples", hop) for hop in range(1, shards)]
    risk, sensitivity, low_sens, high_sens = call(
        functools.partial(moments_body, shards),
        (shape(1, rows * width), flat) + (shape(local_count, width),) * 2,
        (surface, *others, receptor, fixed[0]),
        "moments",
        micros=0.1,
    )
    low, high = exchange_x(low_sens, high_sens)
    edge, inner, beside, run_edge, run_inner = call(
        final_body,
        (
            shape(local_count, 2, width, levels),
            shape(local_count, inside, width, levels),
            rim,
            shape(2, width, levels),
            shape(inside, width, levels),
        ),
        (sensitivity, swap_y(sensitivity), kernel_row),
        "final",
        micros=INNER_COST,
    )
    for step in range(STEPS - 1, 0, -1):
        inner_now, rim_inner, run_inner = call(
            functools.partial(inner_body, step, False),
            (shape(local_count, inside, width, levels), rim, shape(inside, width, levels)),
            (edge, inner, beside, run_inner, *fixed),
            f"inner{step}",
            micros=INNER_COST,
        )
        if step == STEPS - 1:
            low, high = call(
                halo_body, (slab,) * 2, (low, high, kernel_row, rim_inner), "halo", micros=0.1
            )
        edge, to_low, to_high, rim_all, run_edge = call(
            functools.partial(edge_body, step, False, 0),
            (
                shape(local_count, 2, width, levels),
                shape(local_count, width, levels, dtype=BF16),
                shape(local_count, width, levels, dtype=BF16),
                rim,
                shape(2, width, levels),
            ),
            (edge, inner, low, high, beside, run_edge, *fixed, rim_inner),
            f"edge{step}",
            micros=0.4,
        )
        inner = inner_now
        beside = swap_y(rim_all)
        low, high = exchange_x(to_low, to_high)

    share = shape(rows // shards, width, levels)
    pieces = call(
        functools.partial(share_body, shards),
        (share,) * shards,
        (run_edge, run_inner, rim_all),
        "share",
        scratch=[pltpu.VMEM((rows, width, levels), F32)],
        micros=0.1,
    )
    pieces = [pieces[0]] + [rotate(pieces[hop], "samples", hop) for hop in range(1, shards)]
    inner_now, risk_map = call(
        functools.partial(inner_body, 0, True),
        (shape(local_count, inside, width, levels), shape(rows, width)),
        (edge, inner, beside, run_inner, *fixed, risk),
        "inner0",
        micros=INNER_COST,
    )
    initial_adjoint, source_gradient = call(
        functools.partial(edge_body, 0, True, shards),
        (shape(*flags.shape), share),
        (edge, inner, low, high, beside, run_edge, *fixed, *pieces, inner_now),
        "edge0",
        out_specs=(HBM, HBM),
        scratch=[
            pltpu.VMEM((local_count, 2, width, levels), F32),
            pltpu.VMEM(share.shape, F32),
            pltpu.SemaphoreType.DMA((3 * local_count + 1,)),
        ],
        micros=0.4,
    )
    return risk_map, source_gradient, initial_adjoint


def solution(mesh):
    return jax.shard_map(
        on_device,
        mesh=mesh,
        in_specs=(
            P(("groups", "samples")),
            P(),
            P("gx", "gy", None),
            P("gx", "gy", None),
            P(("groups", "samples"), "gx", "gy", None),
            P("gx", "gy"),
            P(),
            P(None, ("groups", "samples"), "gx", "gy", None),
        ),
        out_specs=(
            P(("groups", "gx"), "gy"),
            P(("groups", "gx", "samples"), "gy", None),
            P(("groups", "samples"), "gx", "gy", None),
        ),
        check_vma=False,
    )
```

```python
import functools

import jax
import jax.numpy as jnp
from jax import lax
from jax.experimental import pallas as pl
from jax.experimental.pallas import tpu as pltpu
from jax.sharding import PartitionSpec as P

STEPS = 4
DIFFUSION = 0.05
KURTOSIS_WEIGHT = 1.0

F32 = jnp.float32
BF16 = jnp.bfloat16
VMEM = pl.BlockSpec(memory_space=pltpu.VMEM)
ANY = pl.BlockSpec(memory_space=pl.ANY)
HBM = pl.BlockSpec(memory_space=pltpu.HBM)


def call(body, outs, args, name, out_specs=None, in_specs=None, scratch=(), aliases=None, micros=1.0):
    return pl.pallas_call(
        body,
        name=name,
        out_shape=outs,
        in_specs=in_specs or [VMEM] * len(args),
        out_specs=out_specs or jax.tree.map(lambda _: VMEM, outs),
        scratch_shapes=scratch,
        input_output_aliases=aliases or {},
        compiler_params=pltpu.CompilerParams(vmem_limit_bytes=4 << 20),
        cost_estimate=pl.CostEstimate(
            flops=int(1e6 * micros), bytes_accessed=int(3e6 * micros), transcendentals=0
        ),
    )(*args)


def shape(*dims, dtype=F32):
    return jax.ShapeDtypeStruct(dims, dtype)


def three_parts(value):
    first = value.astype(BF16).astype(F32)
    second = (value - first).astype(BF16).astype(F32)
    third = value - first - second
    return first, second, third


def stack_rows(rows, width):
    index = lax.broadcasted_iota(jnp.int32, (16, width), 0)
    block = jnp.zeros((16, width), F32)
    for position, row in enumerate(rows):
        block = jnp.where(index == position, row, block)
    return block.astype(BF16)


def surface_body(
    states_ref, kernel_ref, flags_ref, gust_ref, reaction_ref,
    surface_ref, kernel_out, flags_out, gust_out, reaction_out, buffer, semaphores
):
    samples, rows, width, levels = buffer.shape
    copies = [
        pltpu.make_async_copy(states_ref.at[STEPS, k], buffer.at[k], semaphores.at[k])
        for k in range(samples)
    ]
    others = ((kernel_ref, kernel_out), (flags_ref, flags_out), (gust_ref, gust_out), (reaction_ref, reaction_out))
    copies += [
        pltpu.make_async_copy(source, target, semaphores.at[samples + i])
        for i, (source, target) in enumerate(others)
    ]
    for copy in copies:
        copy.start()
    copies[samples].wait()
    parts = stack_rows(three_parts(kernel_out[...]), levels)
    for k in range(samples):
        copies[k].wait()
        flat = buffer[k].reshape(rows * width, levels)
        product = lax.dot_general(
            parts, flat, (((1,), (1,)), ((), ())), preferred_element_type=F32
        )
        surface_ref[k : k + 1] = product[0:1] + product[1:2] + product[2:3]
    for copy in copies[samples + 1 :]:
        copy.wait()


def load_body(
    seeds_ref, states_ref, mask_ref, table_ref, _,
    profile_out, stored_out, receptor_out, mask, table, padded, semaphores
):
    _, samples, rows, width, levels = stored_out.shape
    pairs = [(table_ref, table), (mask_ref, mask)]
    pairs += [(states_ref.at[step], stored_out.at[step]) for step in range(STEPS)]
    copies = [
        pltpu.make_async_copy(source, target, semaphores.at[i]) for i, (source, target) in enumerate(pairs)
    ]
    for copy in copies:
        copy.start()
    copies[0].wait()
    for k in range(samples):
        for d in range(3):
            profile_out[k, d : d + 1] = table[d, pl.ds(seeds_ref[k], 1)]
    copies[1].wait()
    padded[...] = jnp.zeros_like(padded)
    padded[:, :width] = mask[...].astype(F32)
    for pair in range(rows // 2):
        receptor_out[:, 2 * width * pair : 2 * width * (pair + 1)] = (
            padded[2 * pair : 2 * pair + 1] + pltpu.roll(padded[2 * pair + 1 : 2 * pair + 2], width, 1)
        )
    for copy in copies[2:]:
        copy.wait()


def moments_body(count, *refs):
    parts, receptor_ref = refs[:count], refs[count]
    risk_ref, sens_ref, low_ref, high_ref = refs[count + 2 :]
    samples, cells = sens_ref.shape
    width = low_ref.shape[1]
    total = samples * count
    fold = lambda values: sum(jnp.sum(value, axis=0, keepdims=True) for value in values) / total
    every = [part[...] for part in parts]
    average = fold(every)
    spread = [value - average for value in every]
    cubed = [value * value * value for value in spread]
    third_moment = fold(cubed)
    fourth_moment = fold([cube * value for cube, value in zip(cubed, spread)])
    receptor = receptor_ref[...]
    risk_ref[...] = receptor * (average + KURTOSIS_WEIGHT * fourth_moment)
    sens = receptor * (1.0 / total + 4.0 * KURTOSIS_WEIGHT / total * (cubed[0] - third_moment))
    sens_ref[...] = sens
    low_ref[...] = sens[:, :width]
    high_ref[...] = pltpu.roll(sens[:, cells - 2 * width :], width, 1)[:, :width]


def outer_rows(row, kernel_rows):
    first, second, third = three_parts(row)
    left = stack_rows((first, first, first, second, second, third), row.shape[1])
    return lax.dot_general(
        left, kernel_rows, (((0,), (0,)), ((), ())), preferred_element_type=F32
    )


def kernel_rows_of(kernel_ref):
    first, second, third = three_parts(kernel_ref[...])
    return stack_rows((first, second, third, first, second, first), kernel_ref.shape[1])


def final_body(sens_ref, beside_ref, kernel_ref, edge_ref, inner_ref, beside_out, run_edge_ref, run_inner_ref):
    samples, inside, width, levels = inner_ref.shape
    rows = inside + 2
    right = kernel_rows_of(kernel_ref)
    total = [jnp.zeros((width, levels), F32)] * rows
    lanes = lax.broadcasted_iota(jnp.int32, (rows, rows * width), 1)
    starts = lax.broadcasted_iota(jnp.int32, (rows, rows * width), 0) * width
    wanted = lanes == starts + jnp.where(lax.axis_index("gy") == 1, width - 1, 0)
    for k in range(samples):
        block = outer_rows(sens_ref[k : k + 1], right)
        for x in range(rows):
            piece = block[x * width : (x + 1) * width]
            if x in (0, rows - 1):
                edge_ref[k, x // (rows - 1)] = piece
            else:
                inner_ref[k, x - 1] = piece
            total[x] = total[x] + piece
        column = jnp.sum(jnp.where(wanted, beside_ref[k : k + 1], 0.0), axis=1, keepdims=True)
        beside_out[k] = column * kernel_ref[...]
    run_edge_ref[0] = total[0]
    run_edge_ref[1] = total[rows - 1]
    for x in range(1, rows - 1):
        run_inner_ref[x - 1] = total[x]


class Plan:
    def __init__(self, levels):
        lane = lax.broadcasted_iota(jnp.int32, (8, levels), 1)
        row = lax.broadcasted_iota(jnp.int32, (8, levels), 0)
        self.below_top = lane < levels - 1
        self.above_base = lane > 0
        self.top_row = row == 7
        self.base_row = row == 0
        self.loss = 1.0 - (
            jnp.where(self.below_top, DIFFUSION, 0.0) + jnp.where(self.above_base, DIFFUSION, 0.0)
        )


def step_row(plan, centre, west, east, low_row, high_row, bits, gust, twice, stored, speeds):
    width, levels = centre.shape
    tiles = width // 8
    first, second, third, whole = speeds
    piece = lambda value, t: value[8 * t : 8 * t + 8]
    parts = [piece(centre, t) for t in range(tiles)]
    up = [pltpu.roll(part, 7, 0) for part in parts] + [jnp.broadcast_to(high_row, (8, levels))]
    down = [jnp.broadcast_to(low_row, (8, levels))] + [pltpu.roll(part, 1, 0) for part in parts]
    result = []
    for t in range(tiles):
        here = parts[t]
        north = jnp.where(plan.top_row, up[t + 1], up[t])
        south = jnp.where(plan.base_row, down[t], down[t + 1])
        above = jnp.where(plan.below_top, pltpu.roll(here, levels - 1, 1), 0.0)
        below = jnp.where(plan.above_base, pltpu.roll(here, 1, 1), 0.0)
        flag = piece(bits, t)
        moved = (
            first * jnp.where((flag & 1) != 0, piece(east, t), piece(west, t))
            + second * jnp.where((flag & 2) != 0, north, south)
            + third * jnp.where((flag & 4) != 0, above, below)
            - whole * here
        )
        result.append(
            here * (plan.loss - piece(twice, t) * piece(stored, t))
            + piece(gust, t) * moved
            + DIFFUSION * (above + below)
        )
    return result


def speeds_of(profile_ref, k, levels):
    rows = [profile_ref[k, d : d + 1] for d in range(3)]
    rows.append(rows[0] + rows[1] + rows[2])
    return [jnp.broadcast_to(row, (8, levels)) for row in rows]


def side_flags(levels):
    side = lax.axis_index("gy")
    ones = jnp.full((1, levels), 1.0, F32)
    return jnp.where(side == 1, ones, 0.0), jnp.where(side == 0, ones, 0.0), side == 1


def inner_body(
    step, last, edge_ref, inner_ref, beside_ref, run_ref, profile_ref, flags_ref, gust_ref, reaction_ref,
    stored_ref, *outs
):
    samples, inside, width, levels = inner_ref.shape
    plan = Plan(levels)
    if last:
        (buffer,) = outs
    else:
        buffer, rim_out, run_out = outs
    low_side, high_side, upper = side_flags(levels)

    def at(k, x):
        return edge_ref[k, x // (inside + 1)] if x in (0, inside + 1) else inner_ref[k, x - 1]

    for x in range(1, inside + 1):
        gust = gust_ref[x]
        twice = 2.0 * reaction_ref[x]
        total = None if last else [run_ref[x - 1, 8 * t : 8 * t + 8] for t in range(width // 8)]
        for k in range(samples):
            halo = beside_ref[k, x : x + 1]
            tiles = step_row(
                plan, at(k, x), at(k, x - 1), at(k, x + 1), halo * low_side, halo * high_side,
                flags_ref[k, x], gust, twice, stored_ref[step, k, x].astype(F32),
                speeds_of(profile_ref, k, levels),
            )
            for t, tile in enumerate(tiles):
                buffer[k, x - 1, 8 * t : 8 * t + 8] = tile
                if not last:
                    total[t] = total[t] + tile
            if not last:
                rim_out[k, x : x + 1] = jnp.where(upper, tiles[0][0:1], tiles[-1][7:8])
        if not last:
            for t, tile in enumerate(total):
                run_out[x - 1, 8 * t : 8 * t + 8] = tile


def edge_body(
    step, last, shards, edge_ref, inner_ref, low_ref, high_ref, beside_ref, run_ref, profile_ref, flags_ref,
    gust_ref, reaction_ref, stored_ref, *outs
):
    samples, inside, width, levels = inner_ref.shape
    plan = Plan(levels)
    copies = []
    if last:
        pieces, (now_ref, risk_ref, target, source_out, risk_out, buffer, source, risk, semaphores) = (
            outs[:shards], outs[shards:]
        )
        for k in range(samples):
            copies.append(
                pltpu.make_async_copy(
                    now_ref.at[k], target.at[k, 1 : inside + 1], semaphores.at[2 * samples + 1 + k]
                )
            )
            copies[-1].start()
        source[...] = sum(piece[...] for piece in pieces)
        for x in range(inside + 2):
            pair = risk_ref[:, 2 * width * (x // 2) : 2 * width * (x // 2 + 1)]
            pair = pair if x % 2 == 0 else pltpu.roll(pair, width, 1)
            risk[x : x + 1] = pair[:, :width]
        copies.append(pltpu.make_async_copy(source, source_out, semaphores.at[2 * samples]))
        copies.append(pltpu.make_async_copy(risk, risk_out, semaphores.at[3 * samples + 1]))
        copies[-2].start()
        copies[-1].start()
    else:
        rim_ref, (buffer, low_out, high_out, rim_out, run_out) = outs[0], outs[-5:]
        rim_out[...] = rim_ref[...]
    low_side, high_side, upper = side_flags(levels)
    right = kernel_rows_of(outs[1]) if low_ref.ndim == 2 else None
    outer = lambda ref, k: (
        ref[k].astype(F32) if right is None else outer_rows(ref[k : k + 1], right)
    )
    for side, x in enumerate((0, inside + 1)):
        gust = gust_ref[x]
        twice = 2.0 * reaction_ref[x]
        total = None if last else [run_ref[side, 8 * t : 8 * t + 8] for t in range(width // 8)]
        for k in range(samples):
            halo = beside_ref[k, x : x + 1]
            if side == 0:
                west, east = outer(low_ref, k), inner_ref[k, 0]
            else:
                west, east = inner_ref[k, inside - 1], outer(high_ref, k)
            tiles = step_row(
                plan, edge_ref[k, side], west, east, halo * low_side, halo * high_side,
                flags_ref[k, x], gust, twice, stored_ref[step, k, x].astype(F32),
                speeds_of(profile_ref, k, levels),
            )
            for t, tile in enumerate(tiles):
                buffer[k, side, 8 * t : 8 * t + 8] = tile
                if not last:
                    total[t] = total[t] + tile
            if not last:
                whole = jnp.concatenate(tiles, axis=0).astype(BF16)
                (low_out if side == 0 else high_out)[k] = whole
                rim_out[k, x : x + 1] = jnp.where(upper, tiles[0][0:1], tiles[-1][7:8])
            if last:
                copies.append(
                    pltpu.make_async_copy(
                        buffer.at[k, side], target.at[k, x], semaphores.at[side * samples + k]
                    )
                )
                copies[-1].start()
        if not last:
            for t, tile in enumerate(total):
                run_out[side, 8 * t : 8 * t + 8] = tile
    for copy in copies:
        copy.wait()


def share_body(shards, edge_ref, inner_ref, _, *outs):
    pieces, full = outs[:shards], outs[shards]
    rows = full.shape[0]
    full[0] = edge_ref[0]
    full[1 : rows - 1] = inner_ref[...]
    full[rows - 1] = edge_ref[1]
    me = lax.axis_index("samples")
    share = rows // shards
    for hop in range(shards):
        owner = lax.rem(me + hop, shards)
        pieces[hop][...] = full[pl.ds(owner * share, share)]


def exchange_x(to_low, to_high):
    count = lax.axis_size("gx")
    forward = [(i, (i + 1) % count) for i in range(count)]
    backward = [(target, source) for source, target in forward]
    return lax.ppermute(to_high, "gx", forward), lax.ppermute(to_low, "gx", backward)


def swap_y(block):
    return lax.ppermute(block, "gy", [(0, 1), (1, 0)])


def rotate(block, axis, hop):
    count = lax.axis_size(axis)
    return lax.ppermute(block, axis, [(i, (i + hop) % count) for i in range(count)])


def on_device(seeds, wind_profiles, gust, reaction, flags, mask, kernel, states):
    local_count, rows, width, levels = flags.shape
    shards = lax.axis_size("samples")
    inside = rows - 2
    rim = shape(local_count, rows, levels)
    flat = shape(local_count, rows * width)
    hold = lambda value: pltpu.with_memory_space_constraint(value, pltpu.HBM)
    states = hold(states)

    surface, kernel_row, *fixed = call(
        surface_body,
        (
            flat,
            shape(1, levels),
            shape(*flags.shape, dtype=flags.dtype),
            shape(*gust.shape),
            shape(*reaction.shape),
        ),
        (states, hold(kernel[None, :]), hold(flags), hold(gust), hold(reaction)),
        "surface",
        in_specs=[HBM] * 5,
        scratch=[
            pltpu.VMEM((local_count, rows, width, levels), BF16),
            pltpu.SemaphoreType.DMA((local_count + 4,)),
        ],
    )
    table = jnp.swapaxes(wind_profiles, 0, 1)
    profile, stored, receptor = call(
        load_body,
        (
            shape(local_count, 3, levels),
            shape(STEPS, *flags.shape, dtype=states.dtype),
            shape(1, rows * width),
        ),
        (seeds, states, hold(mask), hold(table), kernel_row),
        "load",
        in_specs=[pl.BlockSpec(memory_space=pltpu.SMEM)] + [HBM] * 3 + [VMEM],
        scratch=[
            pltpu.VMEM(mask.shape, mask.dtype),
            pltpu.VMEM(table.shape, F32),
            pltpu.VMEM((rows, 2 * width), F32),
            pltpu.SemaphoreType.DMA((STEPS + 2,)),
        ],
    )
    fixed = (profile, *fixed, stored)
    others = [rotate(surface, "samples", hop) for hop in range(1, shards)]
    risk, sensitivity, low_sens, high_sens = call(
        functools.partial(moments_body, shards),
        (shape(1, rows * width), flat) + (shape(local_count, width),) * 2,
        (surface, *others, receptor, profile),
        "moments",
        micros=0.1,
    )
    low, high = exchange_x(low_sens, high_sens)
    edge, inner, beside, run_edge, run_inner = call(
        final_body,
        (
            shape(local_count, 2, width, levels),
            shape(local_count, inside, width, levels),
            rim,
            shape(2, width, levels),
            shape(inside, width, levels),
        ),
        (sensitivity, swap_y(sensitivity), kernel_row),
        "final",
        micros=1.0,
    )
    for step in range(STEPS - 1, 0, -1):
        inner_now, rim_inner, run_inner = call(
            functools.partial(inner_body, step, False),
            (shape(local_count, inside, width, levels), rim, shape(inside, width, levels)),
            (edge, inner, beside, run_inner, *fixed),
            f"inner{step}",
            micros=1.0,
        )
        edge, to_low, to_high, rim_all, run_edge = call(
            functools.partial(edge_body, step, False, 0),
            (
                shape(local_count, 2, width, levels),
                shape(local_count, width, levels, dtype=BF16),
                shape(local_count, width, levels, dtype=BF16),
                rim,
                shape(2, width, levels),
            ),
            (edge, inner, low, high, beside, run_edge, *fixed, rim_inner)
            + ((kernel_row,) if step == STEPS - 1 else ()),
            f"edge{step}",
            micros=0.4,
        )
        inner = inner_now
        beside = swap_y(rim_all)
        low, high = exchange_x(to_low, to_high)

    share = shape(rows // shards, width, levels)
    pieces = call(
        functools.partial(share_body, shards),
        (share,) * shards,
        (run_edge, run_inner, rim_all),
        "share",
        scratch=[pltpu.VMEM((rows, width, levels), F32)],
        micros=0.1,
    )
    pieces = [pieces[0]] + [rotate(pieces[hop], "samples", hop) for hop in range(1, shards)]
    inner_now = call(
        functools.partial(inner_body, 0, True),
        shape(local_count, inside, width, levels),
        (edge, inner, beside, run_inner, *fixed),
        "inner0",
        micros=1.0,
    )
    initial_adjoint, source_gradient, risk_map = call(
        functools.partial(edge_body, 0, True, shards),
        (shape(*flags.shape), share, shape(rows, width)),
        (edge, inner, low, high, beside, run_edge, *fixed, *pieces, inner_now, risk),
        "edge0",
        out_specs=(HBM,) * 3,
        scratch=[
            pltpu.VMEM((local_count, 2, width, levels), F32),
            pltpu.VMEM(share.shape, F32),
            pltpu.VMEM((rows, width), F32),
            pltpu.SemaphoreType.DMA((3 * local_count + 2,)),
        ],
        micros=0.4,
    )
    return risk_map, source_gradient, initial_adjoint


def solution(mesh):
    return jax.shard_map(
        on_device,
        mesh=mesh,
        in_specs=(
            P(("groups", "samples")),
            P(),
            P("gx", "gy", None),
            P("gx", "gy", None),
            P(("groups", "samples"), "gx", "gy", None),
            P("gx", "gy"),
            P(),
            P(None, ("groups", "samples"), "gx", "gy", None),
        ),
        out_specs=(
            P(("groups", "gx"), "gy"),
            P(("groups", "gx", "samples"), "gy", None),
            P(("groups", "samples"), "gx", "gy", None),
        ),
        check_vma=False,
    )
```

```python
import functools

import jax
import jax.numpy as jnp
from jax import lax
from jax.experimental import pallas as pl
from jax.experimental.pallas import tpu as pltpu
from jax.sharding import PartitionSpec as P

STEPS = 4
DIFFUSION = 0.05
KURTOSIS_WEIGHT = 1.0

F32 = jnp.float32
BF16 = jnp.bfloat16
VMEM = pl.BlockSpec(memory_space=pltpu.VMEM)
ANY = pl.BlockSpec(memory_space=pl.ANY)
HBM = pl.BlockSpec(memory_space=pltpu.HBM)


def call(body, outs, args, name, out_specs=None, in_specs=None, scratch=(), aliases=None, micros=1.0):
    return pl.pallas_call(
        body,
        name=name,
        out_shape=outs,
        in_specs=in_specs or [VMEM] * len(args),
        out_specs=out_specs or jax.tree.map(lambda _: VMEM, outs),
        scratch_shapes=scratch,
        input_output_aliases=aliases or {},
        compiler_params=pltpu.CompilerParams(vmem_limit_bytes=4 << 20),
        cost_estimate=pl.CostEstimate(
            flops=int(1e6 * micros), bytes_accessed=int(3e6 * micros), transcendentals=0
        ),
    )(*args)


def shape(*dims, dtype=F32):
    return jax.ShapeDtypeStruct(dims, dtype)


def three_parts(value):
    first = value.astype(BF16).astype(F32)
    second = (value - first).astype(BF16).astype(F32)
    third = value - first - second
    return first, second, third


def stack_rows(rows, width):
    index = lax.broadcasted_iota(jnp.int32, (16, width), 0)
    block = jnp.zeros((16, width), F32)
    for position, row in enumerate(rows):
        block = jnp.where(index == position, row, block)
    return block.astype(BF16)


def surface_body(
    states_ref, kernel_ref, flags_ref, gust_ref, reaction_ref,
    surface_ref, kernel_out, flags_out, gust_out, reaction_out, buffer, semaphores
):
    samples, rows, width, levels = buffer.shape
    copies = [
        pltpu.make_async_copy(states_ref.at[STEPS, k], buffer.at[k], semaphores.at[k])
        for k in range(samples)
    ]
    others = ((kernel_ref, kernel_out), (flags_ref, flags_out), (gust_ref, gust_out), (reaction_ref, reaction_out))
    copies += [
        pltpu.make_async_copy(source, target, semaphores.at[samples + i])
        for i, (source, target) in enumerate(others)
    ]
    for copy in copies:
        copy.start()
    copies[samples].wait()
    parts = stack_rows(three_parts(kernel_out[...]), levels)
    for k in range(samples):
        copies[k].wait()
        flat = buffer[k].reshape(rows * width, levels)
        product = lax.dot_general(
            parts, flat, (((1,), (1,)), ((), ())), preferred_element_type=F32
        )
        surface_ref[k : k + 1] = product[0:1] + product[1:2] + product[2:3]
    for copy in copies[samples + 1 :]:
        copy.wait()


def load_body(
    seeds_ref, states_ref, mask_ref, table_ref, _,
    profile_out, stored_out, receptor_out, mask, table, padded, semaphores
):
    _, samples, rows, width, levels = stored_out.shape
    pairs = [(table_ref, table), (mask_ref, mask)]
    pairs += [(states_ref.at[step], stored_out.at[step]) for step in range(STEPS)]
    copies = [
        pltpu.make_async_copy(source, target, semaphores.at[i]) for i, (source, target) in enumerate(pairs)
    ]
    for copy in copies:
        copy.start()
    copies[0].wait()
    for k in range(samples):
        for d in range(3):
            profile_out[k, d : d + 1] = table[d, pl.ds(seeds_ref[k], 1)]
    copies[1].wait()
    padded[...] = jnp.zeros_like(padded)
    padded[:, :width] = mask[...].astype(F32)
    for pair in range(rows // 2):
        receptor_out[:, 2 * width * pair : 2 * width * (pair + 1)] = (
            padded[2 * pair : 2 * pair + 1] + pltpu.roll(padded[2 * pair + 1 : 2 * pair + 2], width, 1)
        )
    for copy in copies[2:]:
        copy.wait()


def moments_body(count, *refs):
    parts, receptor_ref = refs[:count], refs[count]
    risk_ref, sens_ref, low_ref, high_ref = refs[count + 2 :]
    samples, cells = sens_ref.shape
    width = low_ref.shape[1]
    total = samples * count
    fold = lambda values: sum(jnp.sum(value, axis=0, keepdims=True) for value in values) / total
    every = [part[...] for part in parts]
    average = fold(every)
    spread = [value - average for value in every]
    cubed = [value * value * value for value in spread]
    third_moment = fold(cubed)
    fourth_moment = fold([cube * value for cube, value in zip(cubed, spread)])
    receptor = receptor_ref[...]
    risk_ref[...] = receptor * (average + KURTOSIS_WEIGHT * fourth_moment)
    sens = receptor * (1.0 / total + 4.0 * KURTOSIS_WEIGHT / total * (cubed[0] - third_moment))
    sens_ref[...] = sens
    low_ref[...] = sens[:, :width]
    high_ref[...] = pltpu.roll(sens[:, cells - 2 * width :], width, 1)[:, :width]


def outer_rows(row, kernel_rows):
    first, second, third = three_parts(row)
    left = stack_rows((first, first, first, second, second, third), row.shape[1])
    return lax.dot_general(
        left, kernel_rows, (((0,), (0,)), ((), ())), preferred_element_type=F32
    )


def kernel_rows_of(kernel_ref):
    first, second, third = three_parts(kernel_ref[...])
    return stack_rows((first, second, third, first, second, first), kernel_ref.shape[1])


def final_body(sens_ref, beside_ref, kernel_ref, edge_ref, inner_ref, beside_out, run_edge_ref, run_inner_ref):
    samples, inside, width, levels = inner_ref.shape
    rows = inside + 2
    right = kernel_rows_of(kernel_ref)
    total = [jnp.zeros((width, levels), F32)] * rows
    lanes = lax.broadcasted_iota(jnp.int32, (rows, rows * width), 1)
    starts = lax.broadcasted_iota(jnp.int32, (rows, rows * width), 0) * width
    wanted = lanes == starts + jnp.where(lax.axis_index("gy") == 1, width - 1, 0)
    for k in range(samples):
        block = outer_rows(sens_ref[k : k + 1], right)
        for x in range(rows):
            piece = block[x * width : (x + 1) * width]
            if x in (0, rows - 1):
                edge_ref[k, x // (rows - 1)] = piece
            else:
                inner_ref[k, x - 1] = piece
            total[x] = total[x] + piece
        column = jnp.sum(jnp.where(wanted, beside_ref[k : k + 1], 0.0), axis=1, keepdims=True)
        beside_out[k] = column * kernel_ref[...]
    run_edge_ref[0] = total[0]
    run_edge_ref[1] = total[rows - 1]
    for x in range(1, rows - 1):
        run_inner_ref[x - 1] = total[x]


class Plan:
    def __init__(self, levels):
        lane = lax.broadcasted_iota(jnp.int32, (8, levels), 1)
        row = lax.broadcasted_iota(jnp.int32, (8, levels), 0)
        self.below_top = lane < levels - 1
        self.above_base = lane > 0
        self.top_row = row == 7
        self.base_row = row == 0
        self.loss = 1.0 - (
            jnp.where(self.below_top, DIFFUSION, 0.0) + jnp.where(self.above_base, DIFFUSION, 0.0)
        )


def step_row(plan, centre, west, east, low_row, high_row, bits, gust, twice, stored, speeds):
    width, levels = centre.shape
    tiles = width // 8
    first, second, third, whole = speeds
    piece = lambda value, t: value[8 * t : 8 * t + 8]
    parts = [piece(centre, t) for t in range(tiles)]
    up = [pltpu.roll(part, 7, 0) for part in parts] + [jnp.broadcast_to(high_row, (8, levels))]
    down = [jnp.broadcast_to(low_row, (8, levels))] + [pltpu.roll(part, 1, 0) for part in parts]
    result = []
    for t in range(tiles):
        here = parts[t]
        north = jnp.where(plan.top_row, up[t + 1], up[t])
        south = jnp.where(plan.base_row, down[t], down[t + 1])
        above = jnp.where(plan.below_top, pltpu.roll(here, levels - 1, 1), 0.0)
        below = jnp.where(plan.above_base, pltpu.roll(here, 1, 1), 0.0)
        flag = piece(bits, t)
        moved = (
            first * jnp.where((flag & 1) != 0, piece(east, t), piece(west, t))
            + second * jnp.where((flag & 2) != 0, north, south)
            + third * jnp.where((flag & 4) != 0, above, below)
            - whole * here
        )
        result.append(
            here * (plan.loss - piece(twice, t) * piece(stored, t))
            + piece(gust, t) * moved
            + DIFFUSION * (above + below)
        )
    return result


def speeds_of(profile_ref, k, levels):
    rows = [profile_ref[k, d : d + 1] for d in range(3)]
    rows.append(rows[0] + rows[1] + rows[2])
    return [jnp.broadcast_to(row, (8, levels)) for row in rows]


def side_flags(levels):
    side = lax.axis_index("gy")
    ones = jnp.full((1, levels), 1.0, F32)
    return jnp.where(side == 1, ones, 0.0), jnp.where(side == 0, ones, 0.0), side == 1


def inner_body(
    step, last, edge_ref, inner_ref, beside_ref, run_ref, profile_ref, flags_ref, gust_ref, reaction_ref,
    stored_ref, *outs
):
    samples, inside, width, levels = inner_ref.shape
    plan = Plan(levels)
    if last:
        (buffer,) = outs
    else:
        buffer, rim_out, run_out = outs
    low_side, high_side, upper = side_flags(levels)

    def at(k, x):
        return edge_ref[k, x // (inside + 1)] if x in (0, inside + 1) else inner_ref[k, x - 1]

    for x in range(1, inside + 1):
        gust = gust_ref[x]
        twice = 2.0 * reaction_ref[x]
        total = None if last else [run_ref[x - 1, 8 * t : 8 * t + 8] for t in range(width // 8)]
        for k in range(samples):
            halo = beside_ref[k, x : x + 1]
            tiles = step_row(
                plan, at(k, x), at(k, x - 1), at(k, x + 1), halo * low_side, halo * high_side,
                flags_ref[k, x], gust, twice, stored_ref[step, k, x].astype(F32),
                speeds_of(profile_ref, k, levels),
            )
            for t, tile in enumerate(tiles):
                buffer[k, x - 1, 8 * t : 8 * t + 8] = tile
                if not last:
                    total[t] = total[t] + tile
            if not last:
                rim_out[k, x : x + 1] = jnp.where(upper, tiles[0][0:1], tiles[-1][7:8])
        if not last:
            for t, tile in enumerate(total):
                run_out[x - 1, 8 * t : 8 * t + 8] = tile


def part_body(
    step, edge_ref, inner_ref, beside_ref, profile_ref, flags_ref, gust_ref, reaction_ref, stored_ref, part_ref
):
    samples, inside, width, levels = inner_ref.shape
    plan = Plan(levels)
    low_side, high_side, _ = side_flags(levels)
    empty = jnp.zeros((width, levels), F32)
    for side, x in enumerate((0, inside + 1)):
        gust = gust_ref[x]
        twice = 2.0 * reaction_ref[x]
        for k in range(samples):
            halo = beside_ref[k, x : x + 1]
            west, east = (empty, inner_ref[k, 0]) if side == 0 else (inner_ref[k, inside - 1], empty)
            tiles = step_row(
                plan, edge_ref[k, side], west, east, halo * low_side, halo * high_side,
                flags_ref[k, x], gust, twice, stored_ref[step, k, x].astype(F32),
                speeds_of(profile_ref, k, levels),
            )
            for t, tile in enumerate(tiles):
                part_ref[k, side, 8 * t : 8 * t + 8] = tile


def edge_body(
    last, shards, inside, part_ref, low_ref, high_ref, run_ref, profile_ref, flags_ref, gust_ref, *outs
):
    samples, _, width, levels = part_ref.shape
    copies = []
    if last:
        pieces, (now_ref, risk_ref, target, source_out, risk_out, buffer, source, risk, semaphores) = (
            outs[:shards], outs[shards:]
        )
        for k in range(samples):
            copies.append(
                pltpu.make_async_copy(
                    now_ref.at[k], target.at[k, 1 : inside + 1], semaphores.at[2 * samples + 1 + k]
                )
            )
            copies[-1].start()
        source[...] = sum(piece[...] for piece in pieces)
        for x in range(inside + 2):
            pair = risk_ref[:, 2 * width * (x // 2) : 2 * width * (x // 2 + 1)]
            pair = pair if x % 2 == 0 else pltpu.roll(pair, width, 1)
            risk[x : x + 1] = pair[:, :width]
        copies.append(pltpu.make_async_copy(source, source_out, semaphores.at[2 * samples]))
        copies.append(pltpu.make_async_copy(risk, risk_out, semaphores.at[3 * samples + 1]))
        copies[-2].start()
        copies[-1].start()
    else:
        rim_ref, (buffer, low_out, high_out, rim_out, run_out) = outs[0], outs[-5:]
        rim_out[...] = rim_ref[...]
    upper = side_flags(levels)[2]
    right = kernel_rows_of(outs[1]) if low_ref.ndim == 2 else None
    outer = lambda ref, k: (
        ref[k].astype(F32) if right is None else outer_rows(ref[k : k + 1], right)
    )
    for side, x in enumerate((0, inside + 1)):
        total = None if last else run_ref[side]
        halo_ref = (low_ref, high_ref)[side]
        for k in range(samples):
            toward = (flags_ref[k, x] & 1) != 0
            rate = gust_ref[x] * profile_ref[k, 0:1]
            rate = jnp.where(toward, 0.0, rate) if side == 0 else jnp.where(toward, rate, 0.0)
            now = part_ref[k, side] + rate * outer(halo_ref, k)
            buffer[k, side] = now
            if last:
                copies.append(
                    pltpu.make_async_copy(
                        buffer.at[k, side], target.at[k, x], semaphores.at[side * samples + k]
                    )
                )
                copies[-1].start()
            else:
                total = total + now
                (low_out if side == 0 else high_out)[k] = now.astype(BF16)
                rim_out[k, x : x + 1] = jnp.where(upper, now[0:1], now[width - 1 : width])
        if not last:
            run_out[side] = total
    for copy in copies:
        copy.wait()


def share_body(shards, edge_ref, inner_ref, _, *outs):
    pieces, full = outs[:shards], outs[shards]
    rows = full.shape[0]
    full[0] = edge_ref[0]
    full[1 : rows - 1] = inner_ref[...]
    full[rows - 1] = edge_ref[1]
    me = lax.axis_index("samples")
    share = rows // shards
    for hop in range(shards):
        owner = lax.rem(me + hop, shards)
        pieces[hop][...] = full[pl.ds(owner * share, share)]


def exchange_x(to_low, to_high):
    count = lax.axis_size("gx")
    forward = [(i, (i + 1) % count) for i in range(count)]
    backward = [(target, source) for source, target in forward]
    return lax.ppermute(to_high, "gx", forward), lax.ppermute(to_low, "gx", backward)


def swap_y(block):
    return lax.ppermute(block, "gy", [(0, 1), (1, 0)])


def rotate(block, axis, hop):
    count = lax.axis_size(axis)
    return lax.ppermute(block, axis, [(i, (i + hop) % count) for i in range(count)])


def on_device(seeds, wind_profiles, gust, reaction, flags, mask, kernel, states):
    local_count, rows, width, levels = flags.shape
    shards = lax.axis_size("samples")
    inside = rows - 2
    rim = shape(local_count, rows, levels)
    flat = shape(local_count, rows * width)
    hold = lambda value: pltpu.with_memory_space_constraint(value, pltpu.HBM)
    states = hold(states)

    surface, kernel_row, *fixed = call(
        surface_body,
        (
            flat,
            shape(1, levels),
            shape(*flags.shape, dtype=flags.dtype),
            shape(*gust.shape),
            shape(*reaction.shape),
        ),
        (states, hold(kernel[None, :]), hold(flags), hold(gust), hold(reaction)),
        "surface",
        in_specs=[HBM] * 5,
        scratch=[
            pltpu.VMEM((local_count, rows, width, levels), BF16),
            pltpu.SemaphoreType.DMA((local_count + 4,)),
        ],
    )
    table = jnp.swapaxes(wind_profiles, 0, 1)
    profile, stored, receptor = call(
        load_body,
        (
            shape(local_count, 3, levels),
            shape(STEPS, *flags.shape, dtype=states.dtype),
            shape(1, rows * width),
        ),
        (seeds, states, hold(mask), hold(table), kernel_row),
        "load",
        in_specs=[pl.BlockSpec(memory_space=pltpu.SMEM)] + [HBM] * 3 + [VMEM],
        scratch=[
            pltpu.VMEM(mask.shape, mask.dtype),
            pltpu.VMEM(table.shape, F32),
            pltpu.VMEM((rows, 2 * width), F32),
            pltpu.SemaphoreType.DMA((STEPS + 2,)),
        ],
    )
    fixed = (profile, *fixed, stored)
    others = [rotate(surface, "samples", hop) for hop in range(1, shards)]
    risk, sensitivity, low_sens, high_sens = call(
        functools.partial(moments_body, shards),
        (shape(1, rows * width), flat) + (shape(local_count, width),) * 2,
        (surface, *others, receptor, profile),
        "moments",
        micros=0.1,
    )
    low, high = exchange_x(low_sens, high_sens)
    edge, inner, beside, run_edge, run_inner = call(
        final_body,
        (
            shape(local_count, 2, width, levels),
            shape(local_count, inside, width, levels),
            rim,
            shape(2, width, levels),
            shape(inside, width, levels),
        ),
        (sensitivity, swap_y(sensitivity), kernel_row),
        "final",
        micros=1.0,
    )
    for step in range(STEPS - 1, 0, -1):
        inner_now, rim_inner, run_inner = call(
            functools.partial(inner_body, step, False),
            (shape(local_count, inside, width, levels), rim, shape(inside, width, levels)),
            (edge, inner, beside, run_inner, *fixed),
            f"inner{step}",
            micros=1.0,
        )
        part = call(
            functools.partial(part_body, step),
            shape(local_count, 2, width, levels),
            (edge, inner, beside, *fixed),
            f"part{step}",
            micros=0.4,
        )
        edge, to_low, to_high, rim_all, run_edge = call(
            functools.partial(edge_body, False, 0, inside),
            (
                shape(local_count, 2, width, levels),
                shape(local_count, width, levels, dtype=BF16),
                shape(local_count, width, levels, dtype=BF16),
                rim,
                shape(2, width, levels),
            ),
            (part, low, high, run_edge, *fixed[:3], rim_inner)
            + ((kernel_row,) if step == STEPS - 1 else ()),
            f"edge{step}",
            micros=0.4,
        )
        inner = inner_now
        beside = swap_y(rim_all)
        low, high = exchange_x(to_low, to_high)

    share = shape(rows // shards, width, levels)
    pieces = call(
        functools.partial(share_body, shards),
        (share,) * shards,
        (run_edge, run_inner, rim_all),
        "share",
        scratch=[pltpu.VMEM((rows, width, levels), F32)],
        micros=0.1,
    )
    pieces = [pieces[0]] + [rotate(pieces[hop], "samples", hop) for hop in range(1, shards)]
    inner_now = call(
        functools.partial(inner_body, 0, True),
        shape(local_count, inside, width, levels),
        (edge, inner, beside, run_inner, *fixed),
        "inner0",
        micros=1.0,
    )
    part = call(
        functools.partial(part_body, 0),
        shape(local_count, 2, width, levels),
        (edge, inner, beside, *fixed),
        "part0",
        micros=0.4,
    )
    initial_adjoint, source_gradient, risk_map = call(
        functools.partial(edge_body, True, shards, inside),
        (shape(*flags.shape), share, shape(rows, width)),
        (part, low, high, run_edge, *fixed[:3], *pieces, inner_now, risk),
        "edge0",
        out_specs=(HBM,) * 3,
        scratch=[
            pltpu.VMEM((local_count, 2, width, levels), F32),
            pltpu.VMEM(share.shape, F32),
            pltpu.VMEM((rows, width), F32),
            pltpu.SemaphoreType.DMA((3 * local_count + 2,)),
        ],
        micros=0.4,
    )
    return risk_map, source_gradient, initial_adjoint


def solution(mesh):
    return jax.shard_map(
        on_device,
        mesh=mesh,
        in_specs=(
            P(("groups", "samples")),
            P(),
            P("gx", "gy", None),
            P("gx", "gy", None),
            P(("groups", "samples"), "gx", "gy", None),
            P("gx", "gy"),
            P(),
            P(None, ("groups", "samples"), "gx", "gy", None),
        ),
        out_specs=(
            P(("groups", "gx"), "gy"),
            P(("groups", "gx", "samples"), "gy", None),
            P(("groups", "samples"), "gx", "gy", None),
        ),
        check_vma=False,
    )
```
